32 devices in a mesh: sp: 2 (over x), ep: 16 (over z, y, core).
Axes of the slice: x: 2, y: 2, z: 4, core: 2. Of those that a mesh axis runs over, the one named last changes fastest.
Arguments:
- activations: bfloat16 [16, 8, 3584], P('ep', 'sp'), may hold values from -6 to 6
- out_grad: bfloat16 [16, 8, 3584], P('ep', 'sp'), may hold values from -6 to 6
- route_weights: bfloat16 [16, 8, 8], P('ep', 'sp'), may hold values from 0.019897461 to 0.5
- expert_ids: int32 [16, 8, 8], P('ep', 'sp'), may hold values from 0 to 15, all different within a row; in each aligned block of 8 rows (0 to 7, 8 to 15, ..., all dimensions but the last counted through in order) at most 6 rows name the same one
- w_gate: bfloat16 [16, 3584, 1024], P('ep', None, 'sp'), may hold values from -0.09375 to 0.09375
- w_up: bfloat16 [16, 3584, 1024], P('ep', None, 'sp'), may hold values from -0.09375 to 0.09375
- w_down: bfloat16 [16, 1024, 3584], P('ep', 'sp'), may hold values from -0.1875 to 0.1875
Outputs:
- input_grad: bfloat16 [16, 8, 3584], P('ep', 'sp')
- w_down_grad: float32 [16, 1024, 3584], P('ep', 'sp')
The draws below stay inside these ranges and needn't reach their ends.
Inputs may be any that keep to these rules, and one draw needn't show every extreme that they name: `expert_ids`: each row names 8 different experts. In each aligned block of 8 rows (one token group, the first two dimensions taken together) no expert is named by more than 6 rows, a bound that some block reaches.
All inputs are finite; a program needn't handle non-finite values.
Results may differ from the reference program's by a relative error of at most 0.014.
Values may be sent and summed in bfloat16 or wider, within the bound.
No kernel may reach another device: no remote copies, remote signals or barrier semaphores. Data moves between devices by JAX's collectives and lax.ppermute only.
A program may use at most 64 MiB of HBM per device.

```python
import math
import jax
import jax.numpy as jnp
import numpy as np
from jax import lax

D = 3584
HID = 1024
TOP = 8
TOK_GRP = 8
CAP = 6
N_SP = 2
N_EP = 16


def shard_levels(rng, dims, split, smallest, high):
    loudness = 1.0
    for position, parts in split:
        heights = jax.random.uniform(jax.random.fold_in(jax.random.fold_in(rng, 6), position), (parts,), jnp.float32, smallest / len(split), high / len(split))
        loudness = loudness * jnp.repeat(jnp.exp(heights), dims[position] // parts).reshape((-1,) + (1,) * (len(dims) - 1 - position))
    return loudness


def shared_out(own_key, own, number, rows, count, top, reach, lean):
    order = jax.random.permutation(own_key, count)
    packed, usual = load_shares(count, rows * top, reach, lean, True), load_shares(count, rows * top, reach, lean, False)
    places = jnp.arange(count)

    def named(sizes, rotation):
        used = int((sizes > 0).sum())
        fixed = max(1, used // 4)
        shifted = fixed + (places - fixed + rotation * (used - fixed)) % max(1, count - fixed)
        return jnp.zeros((count,), jnp.int32).at[order[jnp.where(places < fixed, places, shifted)]].set(jnp.asarray(sizes, jnp.int32))

    sizes = jnp.where(number % 4 == 0, named(packed, number // 4), named(usual, number - number // 4 - 1))
    mixed = jax.random.permutation(jax.random.fold_in(own, 3), count)
    giver, receiver = mixed[0:count // 2 * 2:2], mixed[1:count // 2 * 2:2]
    slack = jnp.minimum(sizes[giver] - 1, reach - sizes[receiver]) // 2
    slack = jnp.where((giver == order[0]) | (receiver == order[0]) | (sizes[receiver] == 0), 0, jnp.maximum(slack, 0))
    shifted = jax.random.randint(jax.random.fold_in(own, 4), (count // 2,), 0, 1 << 20) % (slack + 1)
    sizes = sizes.at[giver].add(-shifted).at[receiver].add(shifted)
    items = jnp.searchsorted(jnp.cumsum(sizes), jnp.arange(rows * top), side="right").astype(jnp.int32)
    listing = items.reshape(top, rows).T
    listing = listing[jax.random.permutation(jax.random.fold_in(own, 1), rows)]
    rotation = jax.random.randint(jax.random.fold_in(own, 2), (rows, 1), 0, top)
    return jnp.take_along_axis(listing, (jnp.arange(top)[None, :] + rotation) % top, axis=1)


def load_shares(amount, total, limit, skew, full):
    portions = [(1 << 20) // math.isqrt(standing ** skew) + 1 for standing in range(1, amount + 1)]
    largest = limit if full else min(limit, max(-(-total // amount), total * portions[0] // sum(portions)))
    least = 1 if total - largest >= amount - 1 else 0
    given, rest = [largest] + [least] * (amount - 1), total - largest - least * (amount - 1)
    while rest > 0:
        candidates = [i for i in range(1, amount) if given[i] < largest] or [i for i in range(1, amount) if given[i] < limit]
        mass, remaining = sum([portions[i] for i in candidates]), rest
        for i in candidates:
            extra = min(limit - given[i], max(1, remaining * portions[i] // mass), rest)
            given[i] = given[i] + extra
            rest = rest - extra
    return np.array(given)


def gaussian(key, shape, deviation, limit, pieces=(), kind=jnp.bfloat16):
    values = jax.random.normal(key, shape, jnp.float32) * deviation
    if len(pieces) > 0:
        values = shard_levels(key, shape, pieces, -0.22, 0.18) * values
    return jnp.clip(values, min=-limit, max=limit).astype(kind)


def setup_inputs(seed: int = 0) -> dict:
    seeds = jax.random.split(jax.random.key(seed), 8)
    activations = gaussian(seeds[0], (N_EP, TOK_GRP, D), 1.0, 6.0, ((0, 16), (1, 2)))
    out_grad = gaussian(seeds[1], (N_EP, TOK_GRP, D), 1.0, 6.0, ((0, 16), (1, 2)))
    route_weights = jnp.clip(jnp.exp(math.log(0.5) - 3.224016 * jax.random.uniform(seeds[2], (N_EP, TOK_GRP, TOP), jnp.float32) ** shard_levels(seeds[2], (N_EP, TOK_GRP, TOP), ((0, 16), (1, 2)), -0.2, 0.2)), 0.019897461, 0.5).astype(jnp.bfloat16)
    expert_ids_keys = jax.random.split(jax.random.fold_in(seeds[3], 1), N_EP * TOK_GRP // TOK_GRP)
    expert_ids_turns = jax.random.permutation(jax.random.fold_in(seeds[3], 3), N_EP * TOK_GRP // TOK_GRP)
    expert_ids = jax.vmap(lambda own, number: shared_out(jax.random.fold_in(seeds[3], 2), own, number, TOK_GRP, N_EP, TOP, CAP, 2))(expert_ids_keys, expert_ids_turns).reshape((N_EP, TOK_GRP, TOP))
    w_gate = gaussian(seeds[4], (N_EP, D, HID), D ** -0.5, 0.09375, ((0, 16), (2, 2)))
    w_up = gaussian(seeds[5], (N_EP, D, HID), D ** -0.5, 0.09375, ((0, 16), (2, 2)))
    w_down = gaussian(seeds[6], (N_EP, HID, D), HID ** -0.5, 0.1875, ((0, 16), (1, 2)))
    return dict(activations=activations, out_grad=out_grad, route_weights=route_weights, expert_ids=expert_ids, w_gate=w_gate, w_up=w_up, w_down=w_down)


def expert_terms(rows_in, rows_grad, gate_w, up_w, down_w):
    gate_pre = jnp.dot(rows_in, gate_w, preferred_element_type=jnp.float32)
    up_pre = jnp.dot(rows_in, up_w, preferred_element_type=jnp.float32)
    squash = jax.nn.sigmoid(gate_pre)
    swish = gate_pre * squash
    hidden = (swish * up_pre).astype(jnp.bfloat16)
    hidden_grad = lax.dot_general(rows_grad, down_w, (((1,), (1,)), ((), ())), preferred_element_type=jnp.float32)
    gate_grad = (hidden_grad * up_pre * squash * (1.0 + gate_pre * (1.0 - squash))).astype(jnp.bfloat16)
    up_grad = (hidden_grad * swish).astype(jnp.bfloat16)
    return hidden, gate_grad, up_grad


def slice_part(gate_grad, up_grad, gate_w, up_w):
    first = lax.dot_general(gate_grad, gate_w, (((1,), (1,)), ((), ())), preferred_element_type=jnp.float32)
    second = lax.dot_general(up_grad, up_w, (((1,), (1,)), ((), ())), preferred_element_type=jnp.float32)
    return (first + second).astype(jnp.bfloat16)


def reference(activations, out_grad, route_weights, expert_ids, w_gate, w_up, w_down):
    width = activations.shape[-1]
    flat_in = activations.reshape(-1, width)
    flat_grad = out_grad.reshape(-1, width)
    flat_weight = route_weights.reshape(-1)
    flat_ids = expert_ids.reshape(-1).astype(jnp.int32)
    rows_max = N_EP * CAP
    piece = HID // N_SP

    def expert_pass(carry, item):
        expert, gate_w, up_w, down_w = item
        sort_key = (flat_ids != expert).astype(jnp.int32)
        picked = jnp.argsort(sort_key, stable=True)[:rows_max].astype(jnp.int32)
        live = flat_ids[picked] == expert
        token_row = picked // TOP
        zero_in = jnp.zeros((), flat_in.dtype)
        rows_in = jnp.where(live[:, None], flat_in[token_row], zero_in)
        scaled = (flat_weight[picked].astype(jnp.float32)[:, None] * flat_grad[token_row].astype(jnp.float32)).astype(jnp.bfloat16)
        rows_grad = jnp.where(live[:, None], scaled, jnp.zeros((), scaled.dtype))
        hidden, gate_grad, up_grad = expert_terms(rows_in, rows_grad, gate_w, up_w, down_w)
        total = jnp.zeros((rows_max, width), jnp.float32)
        for slice_idx in range(N_SP):
            lower = slice_idx * piece
            upper = lower + piece
            total = total + slice_part(gate_grad[:, lower:upper], up_grad[:, lower:upper], gate_w[:, lower:upper], up_w[:, lower:upper]).astype(jnp.float32)
        total = jnp.where(live[:, None], total, jnp.zeros((), jnp.float32))
        carry = carry.at[token_row].add(total)
        weight_grad = lax.dot_general(hidden, rows_grad, (((0,), (0,)), ((), ())), preferred_element_type=jnp.float32)
        return carry, weight_grad

    start = jnp.zeros((flat_in.shape[0], width), jnp.float32)
    experts = jnp.arange(N_EP, dtype=jnp.int32)
    summed, weight_grads = lax.scan(expert_pass, start, (experts, w_gate, w_up, w_down))
    return summed.astype(jnp.bfloat16).reshape(activations.shape), weight_grads
```

```python
import jax
import jax.numpy as jnp
from jax import lax
from jax.sharding import PartitionSpec as P

TOP = 8
F32 = jnp.float32
BF16 = jnp.bfloat16


def expert_rows(rows_in, rows_grad, gate_w, up_w, down_w):
    gate_pre = jnp.dot(rows_in, gate_w, preferred_element_type=F32)
    up_pre = jnp.dot(rows_in, up_w, preferred_element_type=F32)
    squash = jax.nn.sigmoid(gate_pre)
    swish = gate_pre * squash
    hidden = (swish * up_pre).astype(BF16)
    hidden_grad = lax.dot_general(
        rows_grad, down_w, (((1,), (1,)), ((), ())), preferred_element_type=F32
    )
    gate_grad = (hidden_grad * up_pre * squash * (1.0 + gate_pre * (1.0 - squash))).astype(BF16)
    up_grad = (hidden_grad * swish).astype(BF16)
    first = lax.dot_general(
        gate_grad, gate_w, (((1,), (1,)), ((), ())), preferred_element_type=F32
    )
    second = lax.dot_general(up_grad, up_w, (((1,), (1,)), ((), ())), preferred_element_type=F32)
    partial_rows = (first + second).astype(BF16)
    weight_grad = lax.dot_general(
        hidden, rows_grad, (((0,), (0,)), ((), ())), preferred_element_type=F32
    )
    return (partial_rows, weight_grad)


def routed(activations, out_grad, route_weights, expert_ids, w_gate, w_up, w_down):
    n_expert = lax.axis_size("ep")
    n_group = lax.axis_size("sp")
    tok_dev = activations.shape[1]
    width = activations.shape[2]
    capacity = max(2, tok_dev * n_group * TOP * 3 // (2 * n_expert))
    group_ids = lax.all_gather(expert_ids, "sp", axis=1, tiled=True)
    group_in, group_grad, group_weight = (
        lax.all_gather(activations, "sp", axis=1, tiled=True),
        lax.all_gather(out_grad, "sp", axis=1, tiled=True),
        lax.all_gather(route_weights, "sp", axis=1, tiled=True),
    )
    tok_grp = group_ids.shape[1]
    slot_expert = group_ids[0].reshape(-1)
    slot_token = jnp.arange(slot_expert.shape[0], dtype=jnp.int32) // TOP
    onehot = (slot_expert[:, None] == jnp.arange(n_expert, dtype=jnp.int32)[None, :]).astype(
        jnp.int32
    )
    before = jnp.cumsum(onehot, axis=0) - onehot
    rank = jnp.sum(before * onehot, axis=1)
    position = slot_expert * capacity + rank
    total_rows = n_expert * capacity
    token_in = group_in[0][slot_token]
    scaled = (
        group_weight[0].reshape(-1).astype(F32)[:, None] * group_grad[0][slot_token].astype(F32)
    ).astype(BF16)
    send_in = (
        jnp.zeros((total_rows, width), BF16)
        .at[position]
        .set(token_in)
        .reshape(n_expert, capacity, width)
    )
    send_grad = (
        jnp.zeros((total_rows, width), BF16)
        .at[position]
        .set(scaled)
        .reshape(n_expert, capacity, width)
    )
    recv_in, recv_grad = (
        lax.all_to_all(send_in, "ep", split_axis=0, concat_axis=0, tiled=True),
        lax.all_to_all(send_grad, "ep", split_axis=0, concat_axis=0, tiled=True),
    )
    flat_in = recv_in.reshape(total_rows, width)
    flat_grad = recv_grad.reshape(total_rows, width)
    partial_rows, weight_grad = expert_rows(flat_in, flat_grad, w_gate[0], w_up[0], w_down[0])
    partial_rows = partial_rows.reshape(n_expert, capacity, width)
    slot_owner = jnp.full((total_rows,), -1, jnp.int32).at[position].set(slot_token)
    owner_match = jnp.arange(tok_grp, dtype=jnp.int32)[:, None] == slot_owner[None, :]
    back_rows = lax.all_to_all(partial_rows, "ep", split_axis=0, concat_axis=0, tiled=True)
    token_sum = jnp.dot(
        owner_match.astype(BF16),
        back_rows.reshape(total_rows, width),
        preferred_element_type=F32,
    )
    own_sum = lax.psum_scatter(token_sum.astype(BF16), "sp", scatter_dimension=0, tiled=True)
    return (own_sum.reshape(1, tok_dev, width), weight_grad[None])


def exchange(value, partner, n_sp, n_ep):
    pairs = [(i, partner(i)) for i in range(n_sp * n_ep)]
    return lax.ppermute(value, ("sp", "ep"), pairs)


def dense(activations, out_grad, route_weights, expert_ids, w_gate, w_up, w_down):
    n_ep = lax.axis_size("ep")
    n_sp = lax.axis_size("sp")
    tok_dev, width = activations.shape[1:]
    swap = lambda value, partner: exchange(value, partner, n_sp, n_ep)
    far = [4 * j for j in range(1, n_ep // 4)][::-1]
    one = lambda i: i ^ n_ep if i & 1 else i ^ 2
    two = lambda i: i ^ 2 if i & 1 else i ^ n_ep
    core = lambda i: i ^ 1

    chosen = expert_ids[0][:, :, None] == jnp.arange(n_ep, dtype=jnp.int32)[None, None, :]
    per_expert = jnp.sum(jnp.where(chosen, route_weights[0].astype(F32)[:, :, None], 0.0), axis=1)
    per_expert = jnp.pad(per_expert, ((0, 0), (0, -n_ep % 128))).astype(BF16)
    mine = jnp.concatenate([activations[0], out_grad[0], per_expert], axis=1)[None]

    parts = {j: swap(mine, lambda i, j=j: i ^ j) for j in far}
    held = jnp.concatenate([mine] + [parts[j] for j in sorted(far)], axis=0)
    held = jnp.concatenate([held, swap(held, one)], axis=0)
    held = jnp.concatenate([held, swap(held, two)], axis=0)
    held = jnp.concatenate([held, swap(held, core)], axis=0)
    blocks = held.shape[0]
    held = held.reshape(blocks * tok_dev, held.shape[2])
    weight = lax.dynamic_slice_in_dim(held[:, 2 * width :], lax.axis_index("ep"), 1, axis=1)
    rows_in = held[:, :width]
    rows_grad = (weight.astype(F32) * held[:, width : 2 * width].astype(F32)).astype(BF16)

    partial_rows, weight_grad = expert_rows(rows_in, rows_grad, w_gate[0], w_up[0], w_down[0])

    total = partial_rows.reshape(blocks, tok_dev, width)
    for partner in (core, two, one):
        half = total.shape[0] // 2
        got = swap(total[half:].astype(BF16), partner)
        total = total[:half].astype(F32) + got.astype(F32)
    sent = total.astype(BF16)
    own = total[0]
    for j in far:
        own = own + swap(sent[j // 4], lambda i, j=j: i ^ j).astype(F32)
    return (own.astype(BF16)[None], weight_grad[None])


def per_device(activations, out_grad, route_weights, expert_ids, w_gate, w_up, w_down):
    n_ep = lax.axis_size("ep")
    n_sp = lax.axis_size("sp")
    tokens = activations.shape[1] * n_sp * n_ep
    rows = n_ep * max(2, activations.shape[1] * n_sp * TOP * 3 // (2 * n_ep))
    few = tokens <= 2 * rows and n_sp == 2 and n_ep >= 8 and n_ep & (n_ep - 1) == 0
    body = dense if few else routed
    return body(activations, out_grad, route_weights, expert_ids, w_gate, w_up, w_down)


def solution(mesh):
    return jax.shard_map(
        per_device,
        mesh=mesh,
        in_specs=(
            P("ep", "sp", None),
            P("ep", "sp", None),
            P("ep", "sp", None),
            P("ep", "sp", None),
            P("ep", None, "sp"),
            P("ep", None, "sp"),
            P("ep", "sp", None),
        ),
        out_specs=(P("ep", "sp", None), P("ep", "sp", None)),
        check_vma=False,
    )
```

```python
import functools

import jax
import jax.numpy as jnp
from jax import lax
from jax.experimental import pallas as pl
from jax.experimental.pallas import tpu as pltpu
from jax.sharding import PartitionSpec as P

TOP = 8
F32 = jnp.float32
BF16 = jnp.bfloat16


def room(mib):
    return pltpu.CompilerParams(vmem_limit_bytes=mib * 2**20)


BUSY = pl.CostEstimate(flops=10**10, transcendentals=0, bytes_accessed=0)
WHOLE = pl.BlockSpec(memory_space=pltpu.VMEM)


def expert_rows(rows_in, rows_grad, gate_w, up_w, down_w):
    gate_pre = jnp.dot(rows_in, gate_w, preferred_element_type=F32)
    up_pre = jnp.dot(rows_in, up_w, preferred_element_type=F32)
    squash = jax.nn.sigmoid(gate_pre)
    swish = gate_pre * squash
    hidden = (swish * up_pre).astype(BF16)
    hidden_grad = lax.dot_general(
        rows_grad, down_w, (((1,), (1,)), ((), ())), preferred_element_type=F32
    )
    gate_grad = (hidden_grad * up_pre * squash * (1.0 + gate_pre * (1.0 - squash))).astype(BF16)
    up_grad = (hidden_grad * swish).astype(BF16)
    first = lax.dot_general(
        gate_grad, gate_w, (((1,), (1,)), ((), ())), preferred_element_type=F32
    )
    second = lax.dot_general(up_grad, up_w, (((1,), (1,)), ((), ())), preferred_element_type=F32)
    partial_rows = (first + second).astype(BF16)
    weight_grad = lax.dot_general(
        hidden, rows_grad, (((0,), (0,)), ((), ())), preferred_element_type=F32
    )
    return (partial_rows, weight_grad)


def routed(activations, out_grad, route_weights, expert_ids, w_gate, w_up, w_down):
    n_expert = lax.axis_size("ep")
    n_group = lax.axis_size("sp")
    tok_dev = activations.shape[1]
    width = activations.shape[2]
    capacity = max(2, tok_dev * n_group * TOP * 3 // (2 * n_expert))
    group_ids = lax.all_gather(expert_ids, "sp", axis=1, tiled=True)
    group_in, group_grad, group_weight = (
        lax.all_gather(activations, "sp", axis=1, tiled=True),
        lax.all_gather(out_grad, "sp", axis=1, tiled=True),
        lax.all_gather(route_weights, "sp", axis=1, tiled=True),
    )
    tok_grp = group_ids.shape[1]
    slot_expert = group_ids[0].reshape(-1)
    slot_token = jnp.arange(slot_expert.shape[0], dtype=jnp.int32) // TOP
    onehot = (slot_expert[:, None] == jnp.arange(n_expert, dtype=jnp.int32)[None, :]).astype(
        jnp.int32
    )
    before = jnp.cumsum(onehot, axis=0) - onehot
    rank = jnp.sum(before * onehot, axis=1)
    position = slot_expert * capacity + rank
    total_rows = n_expert * capacity
    token_in = group_in[0][slot_token]
    scaled = (
        group_weight[0].reshape(-1).astype(F32)[:, None] * group_grad[0][slot_token].astype(F32)
    ).astype(BF16)
    send_in = (
        jnp.zeros((total_rows, width), BF16)
        .at[position]
        .set(token_in)
        .reshape(n_expert, capacity, width)
    )
    send_grad = (
        jnp.zeros((total_rows, width), BF16)
        .at[position]
        .set(scaled)
        .reshape(n_expert, capacity, width)
    )
    recv_in, recv_grad = (
        lax.all_to_all(send_in, "ep", split_axis=0, concat_axis=0, tiled=True),
        lax.all_to_all(send_grad, "ep", split_axis=0, concat_axis=0, tiled=True),
    )
    flat_in = recv_in.reshape(total_rows, width)
    flat_grad = recv_grad.reshape(total_rows, width)
    partial_rows, weight_grad = expert_rows(flat_in, flat_grad, w_gate[0], w_up[0], w_down[0])
    partial_rows = partial_rows.reshape(n_expert, capacity, width)
    slot_owner = jnp.full((total_rows,), -1, jnp.int32).at[position].set(slot_token)
    owner_match = jnp.arange(tok_grp, dtype=jnp.int32)[:, None] == slot_owner[None, :]
    back_rows = lax.all_to_all(partial_rows, "ep", split_axis=0, concat_axis=0, tiled=True)
    token_sum = jnp.dot(
        owner_match.astype(BF16),
        back_rows.reshape(total_rows, width),
        preferred_element_type=F32,
    )
    own_sum = lax.psum_scatter(token_sum.astype(BF16), "sp", scatter_dimension=0, tiled=True)
    return (own_sum.reshape(1, tok_dev, width), weight_grad[None])


def exchange(value, partner, n_sp, n_ep):
    pairs = [(i, partner(i)) for i in range(n_sp * n_ep)]
    return lax.ppermute(value, ("sp", "ep"), pairs)


def rows_kernel(*refs):
    out_ref = refs[-1]
    rows = refs[0].shape[1]
    for n, ref in enumerate(refs[:-1]):
        out_ref[n * rows : (n + 1) * rows, :] = ref[0]


def stack_rows(blocks):
    rows, width = blocks[0].shape[1:]
    return pl.pallas_call(
        rows_kernel,
        out_shape=jax.ShapeDtypeStruct((len(blocks) * rows, width), blocks[0].dtype),
        in_specs=[WHOLE] * len(blocks),
        out_specs=WHOLE,
        compiler_params=room(2),
        cost_estimate=BUSY,
    )(*blocks)


def spread_kernel(grad_in, weight_in, ids_in, out_ref, grad_ref, weight_ref, ids_ref, sem):
    copies = [
        pltpu.make_async_copy(source, target, sem.at[n])
        for n, (source, target) in enumerate(
            ((grad_in, grad_ref), (weight_in, weight_ref), (ids_in, ids_ref))
        )
    ]
    for copy in copies:
        copy.start()
    for copy in copies:
        copy.wait()
    width = grad_ref.shape[2]
    lane = lax.broadcasted_iota(jnp.int32, (grad_ref.shape[1], out_ref.shape[2] - width), 1)
    weight = weight_ref[0].astype(F32)
    spread = jnp.zeros(lane.shape, F32)
    for k in range(ids_ref.shape[2]):
        spread += jnp.where(lane == ids_ref[0, :, k : k + 1], weight[:, k : k + 1], 0.0)
    out_ref[0, :, :width] = grad_ref[0]
    out_ref[0, :, width:] = spread.astype(BF16)


def spread_weights(out_grad, route_weights, expert_ids, n_expert):
    _, tok_dev, width = out_grad.shape
    return pl.pallas_call(
        spread_kernel,
        out_shape=jax.ShapeDtypeStruct((1, tok_dev, width + n_expert + -n_expert % 128), BF16),
        in_specs=[pl.BlockSpec(memory_space=pltpu.HBM)] * 3,
        out_specs=WHOLE,
        scratch_shapes=[
            pltpu.VMEM(out_grad.shape, out_grad.dtype),
            pltpu.VMEM(route_weights.shape, route_weights.dtype),
            pltpu.VMEM(expert_ids.shape, expert_ids.dtype),
            pltpu.SemaphoreType.DMA((3,)),
        ],
        compiler_params=room(2),
        cost_estimate=BUSY,
        name="spread",
    )(*(pltpu.with_memory_space_constraint(x, pltpu.HBM) for x in (out_grad, route_weights, expert_ids)))


def forward_kernel(n, *refs):
    pieces, (gate_w, up_w, gate_by, up_by, hidden_t) = refs[:n], refs[n:]
    rows = jnp.concatenate([piece[...] for piece in pieces], axis=0)
    step = min(256, gate_w.shape[1])
    for c in range(0, gate_w.shape[1], step):
        cols = slice(c, c + step)
        gate_pre = jnp.dot(rows, gate_w[:, cols], preferred_element_type=F32)
        up_pre = jnp.dot(rows, up_w[:, cols], preferred_element_type=F32)
        squash = jax.nn.sigmoid(gate_pre)
        swish = gate_pre * squash
        gate_by[:, cols] = up_pre * squash * (1.0 + gate_pre * (1.0 - squash))
        up_by[:, cols] = swish
        hidden_t[cols, :] = (swish * up_pre).T.astype(BF16)


def backward_kernel(n, width, *refs):
    pieces, (down_w, gate_w, up_w, gate_by, up_by, part, scaled) = refs[:n], refs[n:]
    expert = lax.axis_index("ep")
    start = 0
    for piece in pieces:
        spread = piece[:, width:].astype(F32)
        lane = lax.broadcasted_iota(jnp.int32, spread.shape, 1)
        weight = jnp.sum(jnp.where(lane == expert, spread, 0.0), axis=1, keepdims=True)
        rows = slice(start, start + piece.shape[0])
        scaled[rows, :] = (weight * piece[:, :width].astype(F32)).astype(BF16)
        start += piece.shape[0]
    nt = (((1,), (1,)), ((), ()))
    hidden_grad = lax.dot_general(scaled[...], down_w[...], nt, preferred_element_type=F32)
    gate_grad = (hidden_grad * gate_by[...]).astype(BF16)
    up_grad = (hidden_grad * up_by[...]).astype(BF16)
    step = 512 if width % 512 == 0 else width
    for c in range(0, width, step):
        cols = slice(c, c + step)
        first = lax.dot_general(gate_grad, gate_w[cols, :], nt, preferred_element_type=F32)
        second = lax.dot_general(up_grad, up_w[cols, :], nt, preferred_element_type=F32)
        part[:, cols] = (first + second).astype(BF16)


def dense(activations, out_grad, route_weights, expert_ids, w_gate, w_up, w_down):
    n_ep = lax.axis_size("ep")
    n_sp = lax.axis_size("sp")
    tok_dev, width = activations.shape[1:]
    units = w_gate.shape[2]

    def swap(value, partner):
        return exchange(value, partner, n_sp, n_ep)

    far = [4 * j for j in range(1, n_ep // 4)][::-1]
    one = lambda i: i ^ n_ep if i & 1 else i ^ 2
    two = lambda i: i ^ 2 if i & 1 else i ^ n_ep
    core = lambda i: i ^ 1

    def gather(mine):
        parts = {j: swap(mine, lambda i, j=j: i ^ j) for j in far}
        column = stack_rows([mine] + [parts[j] for j in sorted(far)])
        half = jnp.concatenate([column, swap(column, one)], axis=0)
        other = swap(half, core)
        rest = swap(half, two)
        return [half, rest, other, swap(rest, core)]

    rows_in = gather(activations)
    gradients = spread_weights(out_grad, route_weights, expert_ids, n_ep)
    rows_grad = gather(gradients)
    gate_w, up_w, down_w = w_gate[0], w_up[0], w_down[0]
    rows = sum(piece.shape[0] for piece in rows_in)
    n = len(rows_in)

    gate_by, up_by, hidden_t = pl.pallas_call(
        functools.partial(forward_kernel, n),
        out_shape=(
            jax.ShapeDtypeStruct((rows, units), F32),
            jax.ShapeDtypeStruct((rows, units), F32),
            jax.ShapeDtypeStruct((units, rows), BF16),
        ),
        in_specs=[WHOLE] * (n + 2),
        out_specs=(WHOLE,) * 3,
        compiler_params=room(16),
        name="forward",
    )(*rows_in, gate_w, up_w)
    part, scaled = pl.pallas_call(
        functools.partial(backward_kernel, n, width),
        out_shape=(
            jax.ShapeDtypeStruct((rows, width), BF16),
            jax.ShapeDtypeStruct((rows, width), BF16),
        ),
        in_specs=[WHOLE] * (n + 5),
        out_specs=(WHOLE,) * 2,
        compiler_params=room(24),
        name="backward",
    )(*rows_grad, down_w, gate_w, up_w, gate_by, up_by)
    weight_grad = jnp.dot(hidden_t, scaled, preferred_element_type=F32)

    total = part
    for partner in (core, two, one):
        half = total.shape[0] // 2
        got = swap(total[half:].astype(BF16), partner)
        total = total[:half].astype(F32) + got.astype(F32)
    sent = total.astype(BF16)
    own = total[:tok_dev]
    for j in far:
        block = sent[j // 4 * tok_dev : (j // 4 + 1) * tok_dev]
        own = own + swap(block, lambda i, j=j: i ^ j).astype(F32)
    return (own.astype(BF16)[None], weight_grad[None])


def per_device(activations, out_grad, route_weights, expert_ids, w_gate, w_up, w_down):
    n_ep = lax.axis_size("ep")
    n_sp = lax.axis_size("sp")
    tokens = activations.shape[1] * n_sp * n_ep
    rows = n_ep * max(2, activations.shape[1] * n_sp * TOP * 3 // (2 * n_ep))
    few = tokens <= 2 * rows and n_sp == 2 and n_ep >= 8 and n_ep & (n_ep - 1) == 0
    if not few:
        return routed(activations, out_grad, route_weights, expert_ids, w_gate, w_up, w_down)
    return dense(activations, out_grad, route_weights, expert_ids, w_gate, w_up, w_down)


def solution(mesh):
    return jax.shard_map(
        per_device,
        mesh=mesh,
        in_specs=(
            P("ep", "sp", None),
            P("ep", "sp", None),
            P("ep", "sp", None),
            P("ep", "sp", None),
            P("ep", None, "sp"),
            P("ep", None, "sp"),
            P("ep", "sp", None),
        ),
        out_specs=(P("ep", "sp", None), P("ep", "sp", None)),
        check_vma=False,
    )
```

```python
import functools

import jax
import jax.numpy as jnp
from jax import lax
from jax.experimental import pallas as pl
from jax.experimental.pallas import tpu as pltpu
from jax.sharding import PartitionSpec as P

TOP = 8
F32 = jnp.float32
BF16 = jnp.bfloat16


def room(mib):
    return pltpu.CompilerParams(vmem_limit_bytes=mib * 2**20)


BUSY = pl.CostEstimate(flops=10**10, transcendentals=0, bytes_accessed=0)
QUICK = pl.CostEstimate(flops=10**6, transcendentals=0, bytes_accessed=0)
WHOLE = pl.BlockSpec(memory_space=pltpu.VMEM)


def expert_rows(rows_in, rows_grad, gate_w, up_w, down_w):
    gate_pre = jnp.dot(rows_in, gate_w, preferred_element_type=F32)
    up_pre = jnp.dot(rows_in, up_w, preferred_element_type=F32)
    squash = jax.nn.sigmoid(gate_pre)
    swish = gate_pre * squash
    hidden = (swish * up_pre).astype(BF16)
    hidden_grad = lax.dot_general(
        rows_grad, down_w, (((1,), (1,)), ((), ())), preferred_element_type=F32
    )
    gate_grad = (hidden_grad * up_pre * squash * (1.0 + gate_pre * (1.0 - squash))).astype(BF16)
    up_grad = (hidden_grad * swish).astype(BF16)
    first = lax.dot_general(
        gate_grad, gate_w, (((1,), (1,)), ((), ())), preferred_element_type=F32
    )
    second = lax.dot_general(up_grad, up_w, (((1,), (1,)), ((), ())), preferred_element_type=F32)
    partial_rows = (first + second).astype(BF16)
    weight_grad = lax.dot_general(
        hidden, rows_grad, (((0,), (0,)), ((), ())), preferred_element_type=F32
    )
    return (partial_rows, weight_grad)


def routed(activations, out_grad, route_weights, expert_ids, w_gate, w_up, w_down):
    n_expert = lax.axis_size("ep")
    n_group = lax.axis_size("sp")
    tok_dev = activations.shape[1]
    width = activations.shape[2]
    capacity = max(2, tok_dev * n_group * TOP * 3 // (2 * n_expert))
    group_ids = lax.all_gather(expert_ids, "sp", axis=1, tiled=True)
    group_in, group_grad, group_weight = (
        lax.all_gather(activations, "sp", axis=1, tiled=True),
        lax.all_gather(out_grad, "sp", axis=1, tiled=True),
        lax.all_gather(route_weights, "sp", axis=1, tiled=True),
    )
    tok_grp = group_ids.shape[1]
    slot_expert = group_ids[0].reshape(-1)
    slot_token = jnp.arange(slot_expert.shape[0], dtype=jnp.int32) // TOP
    onehot = (slot_expert[:, None] == jnp.arange(n_expert, dtype=jnp.int32)[None, :]).astype(
        jnp.int32
    )
    before = jnp.cumsum(onehot, axis=0) - onehot
    rank = jnp.sum(before * onehot, axis=1)
    position = slot_expert * capacity + rank
    total_rows = n_expert * capacity
    token_in = group_in[0][slot_token]
    scaled = (
        group_weight[0].reshape(-1).astype(F32)[:, None] * group_grad[0][slot_token].astype(F32)
    ).astype(BF16)
    send_in = (
        jnp.zeros((total_rows, width), BF16)
        .at[position]
        .set(token_in)
        .reshape(n_expert, capacity, width)
    )
    send_grad = (
        jnp.zeros((total_rows, width), BF16)
        .at[position]
        .set(scaled)
        .reshape(n_expert, capacity, width)
    )
    recv_in, recv_grad = (
        lax.all_to_all(send_in, "ep", split_axis=0, concat_axis=0, tiled=True),
        lax.all_to_all(send_grad, "ep", split_axis=0, concat_axis=0, tiled=True),
    )
    flat_in = recv_in.reshape(total_rows, width)
    flat_grad = recv_grad.reshape(total_rows, width)
    partial_rows, weight_grad = expert_rows(flat_in, flat_grad, w_gate[0], w_up[0], w_down[0])
    partial_rows = partial_rows.reshape(n_expert, capacity, width)
    slot_owner = jnp.full((total_rows,), -1, jnp.int32).at[position].set(slot_token)
    owner_match = jnp.arange(tok_grp, dtype=jnp.int32)[:, None] == slot_owner[None, :]
    back_rows = lax.all_to_all(partial_rows, "ep", split_axis=0, concat_axis=0, tiled=True)
    token_sum = jnp.dot(
        owner_match.astype(BF16),
        back_rows.reshape(total_rows, width),
        preferred_element_type=F32,
    )
    own_sum = lax.psum_scatter(token_sum.astype(BF16), "sp", scatter_dimension=0, tiled=True)
    return (own_sum.reshape(1, tok_dev, width), weight_grad[None])


def exchange(value, partner, n_sp, n_ep):
    pairs = [(i, partner(i)) for i in range(n_sp * n_ep)]
    return lax.ppermute(value, ("sp", "ep"), pairs)


def pack_kernel(in_ref, grad_ref, weight_ref, ids_ref, out_ref, rows, weights, ids, sem):
    tok_dev, width = in_ref.shape[1:]
    copies = [
        pltpu.make_async_copy(source, target, sem.at[n])
        for n, (source, target) in enumerate(
            (
                (weight_ref, weights),
                (ids_ref, ids),
                (in_ref.at[0], rows.at[0]),
                (grad_ref.at[0], rows.at[1]),
            )
        )
    ]
    for copy in copies:
        copy.start()
    for copy in copies:
        copy.wait()
    lane = lax.broadcasted_iota(jnp.int32, (tok_dev, out_ref.shape[1] - width), 1)
    weight = weights[0].astype(F32)
    spread = jnp.zeros(lane.shape, F32)
    for k in range(ids.shape[2]):
        spread += jnp.where(lane == ids[0, :, k : k + 1], weight[:, k : k + 1], 0.0)
    out_ref[:tok_dev, :width] = rows[0]
    out_ref[:tok_dev, width:] = jnp.zeros(lane.shape, BF16)
    out_ref[tok_dev:, :width] = rows[1]
    out_ref[tok_dev:, width:] = spread.astype(BF16)


def pack(activations, out_grad, route_weights, expert_ids, n_expert):
    _, tok_dev, width = out_grad.shape
    operands = (activations, out_grad, route_weights, expert_ids)
    return pl.pallas_call(
        pack_kernel,
        out_shape=jax.ShapeDtypeStruct((2 * tok_dev, width + n_expert + -n_expert % 128), BF16),
        in_specs=[pl.BlockSpec(memory_space=pltpu.HBM)] * 4,
        out_specs=WHOLE,
        scratch_shapes=[
            pltpu.VMEM((2, tok_dev, width), BF16),
            pltpu.VMEM(route_weights.shape, route_weights.dtype),
            pltpu.VMEM(expert_ids.shape, expert_ids.dtype),
            pltpu.SemaphoreType.DMA((4,)),
        ],
        compiler_params=room(2),
        cost_estimate=QUICK,
        name="pack",
    )(*(pltpu.with_memory_space_constraint(x, pltpu.HBM) for x in operands))


def stack_kernel(*refs):
    in_ref, grad_ref = refs[-2:]
    rows, width = refs[0].shape[0] // 2, in_ref.shape[1]
    for n, ref in enumerate(refs[:-2]):
        block = slice(n * rows, (n + 1) * rows)
        in_ref[block, :] = ref[:rows, :width]
        grad_ref[block, :] = ref[rows:, :]


def stack(blocks, width):
    rows, wide = blocks[0].shape
    rows = len(blocks) * rows // 2
    return pl.pallas_call(
        stack_kernel,
        out_shape=(
            jax.ShapeDtypeStruct((rows, width), BF16),
            jax.ShapeDtypeStruct((rows, wide), BF16),
        ),
        in_specs=[WHOLE] * len(blocks),
        out_specs=(WHOLE,) * 2,
        compiler_params=room(2),
        cost_estimate=BUSY,
        name="stack",
    )(*blocks)


def forward_kernel(n, *refs):
    pieces, (gate_w, up_w, gate_by, up_by, hidden_t) = refs[:n], refs[n:]
    rows = jnp.concatenate([piece[...] for piece in pieces], axis=0)
    step = min(256, gate_w.shape[1])
    for c in range(0, gate_w.shape[1], step):
        cols = slice(c, c + step)
        gate_pre = jnp.dot(rows, gate_w[:, cols], preferred_element_type=F32)
        up_pre = jnp.dot(rows, up_w[:, cols], preferred_element_type=F32)
        squash = jax.nn.sigmoid(gate_pre)
        swish = gate_pre * squash
        gate_by[:, cols] = up_pre * squash * (1.0 + gate_pre * (1.0 - squash))
        up_by[:, cols] = swish
        hidden_t[cols, :] = (swish * up_pre).T.astype(BF16)


def backward_kernel(n, width, *refs):
    pieces, (down_w, gate_w, up_w, gate_by, up_by, part, scaled) = refs[:n], refs[n:]
    expert = lax.axis_index("ep")
    start = 0
    for piece in pieces:
        spread = piece[:, width:].astype(F32)
        lane = lax.broadcasted_iota(jnp.int32, spread.shape, 1)
        weight = jnp.sum(jnp.where(lane == expert, spread, 0.0), axis=1, keepdims=True)
        rows = slice(start, start + piece.shape[0])
        scaled[rows, :] = (weight * piece[:, :width].astype(F32)).astype(BF16)
        start += piece.shape[0]
    nt = (((1,), (1,)), ((), ()))
    hidden_grad = lax.dot_general(scaled[...], down_w[...], nt, preferred_element_type=F32)
    gate_grad = (hidden_grad * gate_by[...]).astype(BF16)
    up_grad = (hidden_grad * up_by[...]).astype(BF16)
    step = 512 if width % 512 == 0 else width
    for c in range(0, width, step):
        cols = slice(c, c + step)
        first = lax.dot_general(gate_grad, gate_w[cols, :], nt, preferred_element_type=F32)
        second = lax.dot_general(up_grad, up_w[cols, :], nt, preferred_element_type=F32)
        part[:, cols] = (first + second).astype(BF16)


def dense(activations, out_grad, route_weights, expert_ids, w_gate, w_up, w_down):
    n_ep = lax.axis_size("ep")
    n_sp = lax.axis_size("sp")
    tok_dev, width = activations.shape[1:]
    units = w_gate.shape[2]

    def swap(value, partner):
        return exchange(value, partner, n_sp, n_ep)

    far = [4 * j for j in range(1, n_ep // 4)][::-1]
    one = lambda i: i ^ n_ep if i & 1 else i ^ 2
    two = lambda i: i ^ 2 if i & 1 else i ^ n_ep
    core = lambda i: i ^ 1

    def gather(column):
        half = jnp.concatenate([column, swap(column, one)], axis=0)
        other = swap(half, core)
        rest = swap(half, two)
        return [half, rest, other, swap(rest, core)]

    mine = pack(activations, out_grad, route_weights, expert_ids, n_ep)
    blocks = {j: swap(mine, lambda i, j=j: i ^ j) for j in far}
    column_in, column_grad = stack([mine] + [blocks[j] for j in sorted(far)], width)
    rows_in = gather(column_in)
    rows_grad = gather(column_grad)
    gate_w, up_w, down_w = w_gate[0], w_up[0], w_down[0]
    rows = sum(piece.shape[0] for piece in rows_in)
    n = len(rows_in)

    gate_by, up_by, hidden_t = pl.pallas_call(
        functools.partial(forward_kernel, n),
        out_shape=(
            jax.ShapeDtypeStruct((rows, units), F32),
            jax.ShapeDtypeStruct((rows, units), F32),
            jax.ShapeDtypeStruct((units, rows), BF16),
        ),
        in_specs=[WHOLE] * (n + 2),
        out_specs=(WHOLE,) * 3,
        compiler_params=room(16),
        cost_estimate=QUICK,
        name="forward",
    )(*rows_in, gate_w, up_w)
    part, scaled = pl.pallas_call(
        functools.partial(backward_kernel, n, width),
        out_shape=(
            jax.ShapeDtypeStruct((rows, width), BF16),
            jax.ShapeDtypeStruct((rows, width), BF16),
        ),
        in_specs=[WHOLE] * (n + 5),
        out_specs=(WHOLE,) * 2,
        compiler_params=room(24),
        cost_estimate=QUICK,
        name="backward",
    )(*rows_grad, down_w, gate_w, up_w, gate_by, up_by)
    weight_grad = jnp.dot(hidden_t, scaled, preferred_element_type=F32)

    total = part
    for partner in (core, two, one):
        half = total.shape[0] // 2
        got = swap(total[half:].astype(BF16), partner)
        total = total[:half].astype(F32) + got.astype(F32)
    sent = total.astype(BF16)
    own = total[:tok_dev]
    for j in far:
        block = sent[j // 4 * tok_dev : (j // 4 + 1) * tok_dev]
        own = own + swap(block, lambda i, j=j: i ^ j).astype(F32)
    return (own.astype(BF16)[None], weight_grad[None])


def per_device(activations, out_grad, route_weights, expert_ids, w_gate, w_up, w_down):
    n_ep = lax.axis_size("ep")
    n_sp = lax.axis_size("sp")
    tokens = activations.shape[1] * n_sp * n_ep
    rows = n_ep * max(2, activations.shape[1] * n_sp * TOP * 3 // (2 * n_ep))
    few = tokens <= 2 * rows and n_sp == 2 and n_ep >= 8 and n_ep & (n_ep - 1) == 0
    if not few:
        return routed(activations, out_grad, route_weights, expert_ids, w_gate, w_up, w_down)
    return dense(activations, out_grad, route_weights, expert_ids, w_gate, w_up, w_down)


def solution(mesh):
    return jax.shard_map(
        per_device,
        mesh=mesh,
        in_specs=(
            P("ep", "sp", None),
            P("ep", "sp", None),
            P("ep", "sp", None),
            P("ep", "sp", None),
            P("ep", None, "sp"),
            P("ep", None, "sp"),
            P("ep", "sp", None),
        ),
        out_specs=(P("ep", "sp", None), P("ep", "sp", None)),
        check_vma=False,
    )
```

```python
import functools

import jax
import jax.numpy as jnp
from jax import lax
from jax.experimental import pallas as pl
from jax.experimental.pallas import tpu as pltpu
from jax.sharding import PartitionSpec as P

TOP = 8
TURN = 512
F32 = jnp.float32
BF16 = jnp.bfloat16


def room(mib):
    return pltpu.CompilerParams(vmem_limit_bytes=mib * 2**20)


BUSY = pl.CostEstimate(flops=10**10, transcendentals=0, bytes_accessed=0)
QUICK = pl.CostEstimate(flops=10**6, transcendentals=0, bytes_accessed=0)
WHOLE = pl.BlockSpec(memory_space=pltpu.VMEM)


def expert_rows(rows_in, rows_grad, gate_w, up_w, down_w):
    gate_pre = jnp.dot(rows_in, gate_w, preferred_element_type=F32)
    up_pre = jnp.dot(rows_in, up_w, preferred_element_type=F32)
    squash = jax.nn.sigmoid(gate_pre)
    swish = gate_pre * squash
    hidden = (swish * up_pre).astype(BF16)
    hidden_grad = lax.dot_general(
        rows_grad, down_w, (((1,), (1,)), ((), ())), preferred_element_type=F32
    )
    gate_grad = (hidden_grad * up_pre * squash * (1.0 + gate_pre * (1.0 - squash))).astype(BF16)
    up_grad = (hidden_grad * swish).astype(BF16)
    first = lax.dot_general(
        gate_grad, gate_w, (((1,), (1,)), ((), ())), preferred_element_type=F32
    )
    second = lax.dot_general(up_grad, up_w, (((1,), (1,)), ((), ())), preferred_element_type=F32)
    partial_rows = (first + second).astype(BF16)
    weight_grad = lax.dot_general(
        hidden, rows_grad, (((0,), (0,)), ((), ())), preferred_element_type=F32
    )
    return (partial_rows, weight_grad)


def routed(activations, out_grad, route_weights, expert_ids, w_gate, w_up, w_down):
    n_expert = lax.axis_size("ep")
    n_group = lax.axis_size("sp")
    tok_dev = activations.shape[1]
    width = activations.shape[2]
    capacity = max(2, tok_dev * n_group * TOP * 3 // (2 * n_expert))
    group_ids = lax.all_gather(expert_ids, "sp", axis=1, tiled=True)
    group_in, group_grad, group_weight = (
        lax.all_gather(activations, "sp", axis=1, tiled=True),
        lax.all_gather(out_grad, "sp", axis=1, tiled=True),
        lax.all_gather(route_weights, "sp", axis=1, tiled=True),
    )
    tok_grp = group_ids.shape[1]
    slot_expert = group_ids[0].reshape(-1)
    slot_token = jnp.arange(slot_expert.shape[0], dtype=jnp.int32) // TOP
    onehot = (slot_expert[:, None] == jnp.arange(n_expert, dtype=jnp.int32)[None, :]).astype(
        jnp.int32
    )
    before = jnp.cumsum(onehot, axis=0) - onehot
    rank = jnp.sum(before * onehot, axis=1)
    position = slot_expert * capacity + rank
    total_rows = n_expert * capacity
    token_in = group_in[0][slot_token]
    scaled = (
        group_weight[0].reshape(-1).astype(F32)[:, None] * group_grad[0][slot_token].astype(F32)
    ).astype(BF16)
    send_in = (
        jnp.zeros((total_rows, width), BF16)
        .at[position]
        .set(token_in)
        .reshape(n_expert, capacity, width)
    )
    send_grad = (
        jnp.zeros((total_rows, width), BF16)
        .at[position]
        .set(scaled)
        .reshape(n_expert, capacity, width)
    )
    recv_in, recv_grad = (
        lax.all_to_all(send_in, "ep", split_axis=0, concat_axis=0, tiled=True),
        lax.all_to_all(send_grad, "ep", split_axis=0, concat_axis=0, tiled=True),
    )
    flat_in = recv_in.reshape(total_rows, width)
    flat_grad = recv_grad.reshape(total_rows, width)
    partial_rows, weight_grad = expert_rows(flat_in, flat_grad, w_gate[0], w_up[0], w_down[0])
    partial_rows = partial_rows.reshape(n_expert, capacity, width)
    slot_owner = jnp.full((total_rows,), -1, jnp.int32).at[position].set(slot_token)
    owner_match = jnp.arange(tok_grp, dtype=jnp.int32)[:, None] == slot_owner[None, :]
    back_rows = lax.all_to_all(partial_rows, "ep", split_axis=0, concat_axis=0, tiled=True)
    token_sum = jnp.dot(
        owner_match.astype(BF16),
        back_rows.reshape(total_rows, width),
        preferred_element_type=F32,
    )
    own_sum = lax.psum_scatter(token_sum.astype(BF16), "sp", scatter_dimension=0, tiled=True)
    return (own_sum.reshape(1, tok_dev, width), weight_grad[None])


def back_order(far):
    return far[:1] + far[-1:] + far[1:-1] if len(far) > 1 else far


def exchange(value, partner, n_sp, n_ep):
    pairs = [(i, partner(i)) for i in range(n_sp * n_ep)]
    return lax.ppermute(value, ("sp", "ep"), pairs)


def pack_kernel(in_ref, grad_ref, weight_ref, ids_ref, out_ref, rows, weights, ids, sem):
    tok_dev, width = in_ref.shape[1:]
    copies = [
        pltpu.make_async_copy(source, target, sem.at[n])
        for n, (source, target) in enumerate(
            (
                (weight_ref, weights),
                (ids_ref, ids),
                (in_ref.at[0], rows.at[0]),
                (grad_ref.at[0], rows.at[1]),
            )
        )
    ]
    for copy in copies:
        copy.start()
    for copy in copies:
        copy.wait()
    lane = lax.broadcasted_iota(jnp.int32, (tok_dev, out_ref.shape[1] - width), 1)
    weight = weights[0].astype(F32)
    spread = jnp.zeros(lane.shape, F32)
    for k in range(ids.shape[2]):
        spread += jnp.where(lane == ids[0, :, k : k + 1], weight[:, k : k + 1], 0.0)
    out_ref[:tok_dev, :width] = rows[0]
    out_ref[:tok_dev, width:] = jnp.zeros(lane.shape, BF16)
    out_ref[tok_dev:, :width] = rows[1]
    out_ref[tok_dev:, width:] = spread.astype(BF16)


def pack(activations, out_grad, route_weights, expert_ids, n_expert):
    _, tok_dev, width = out_grad.shape
    operands = (activations, out_grad, route_weights, expert_ids)
    return pl.pallas_call(
        pack_kernel,
        out_shape=jax.ShapeDtypeStruct((2 * tok_dev, width + n_expert + -n_expert % 128), BF16),
        in_specs=[pl.BlockSpec(memory_space=pltpu.HBM)] * 4,
        out_specs=WHOLE,
        scratch_shapes=[
            pltpu.VMEM((2, tok_dev, width), BF16),
            pltpu.VMEM(route_weights.shape, route_weights.dtype),
            pltpu.VMEM(expert_ids.shape, expert_ids.dtype),
            pltpu.SemaphoreType.DMA((4,)),
        ],
        compiler_params=room(2),
        cost_estimate=BUSY,
        name="pack",
    )(*(pltpu.with_memory_space_constraint(x, pltpu.HBM) for x in operands))


def stack_kernel(*refs):
    in_ref, grad_ref = refs[-2:]
    rows, width = refs[0].shape[0] // 2, in_ref.shape[1]
    for n, ref in enumerate(refs[:-2]):
        block = slice(n * rows, (n + 1) * rows)
        in_ref[block, :] = ref[:rows, :width]
        grad_ref[block, :] = ref[rows:, :]


def stack(blocks, width):
    rows, wide = blocks[0].shape
    rows = len(blocks) * rows // 2
    return pl.pallas_call(
        stack_kernel,
        out_shape=(
            jax.ShapeDtypeStruct((rows, width), BF16),
            jax.ShapeDtypeStruct((rows, wide), BF16),
        ),
        in_specs=[WHOLE] * len(blocks),
        out_specs=(WHOLE,) * 2,
        compiler_params=room(2),
        cost_estimate=QUICK,
        name="stack",
    )(*blocks)


def turn_kernel(n, *refs):
    for source, target in zip(refs[:n], refs[n:]):
        for c in range(0, source.shape[0], TURN):
            rows = slice(c, min(c + TURN, source.shape[0]))
            target[:, rows] = source[rows, :].T


def turn(*weights):
    n = len(weights)
    return pl.pallas_call(
        functools.partial(turn_kernel, n),
        out_shape=[jax.ShapeDtypeStruct(w.shape[::-1], w.dtype) for w in weights],
        in_specs=[WHOLE] * n,
        out_specs=[WHOLE] * n,
        compiler_params=room(16),
        cost_estimate=QUICK,
        name="turn",
    )(*weights)


def forward_kernel(n, *refs):
    pieces, (gate_w, up_w, gate_by, up_by, hidden_t) = refs[:n], refs[n:]
    rows = jnp.concatenate([piece[...] for piece in pieces], axis=0)
    step = min(256, gate_w.shape[1])
    for c in range(0, gate_w.shape[1], step):
        cols = slice(c, c + step)
        gate_pre = jnp.dot(rows, gate_w[:, cols], preferred_element_type=F32)
        up_pre = jnp.dot(rows, up_w[:, cols], preferred_element_type=F32)
        squash = jax.nn.sigmoid(gate_pre)
        swish = gate_pre * squash
        gate_by[:, cols] = up_pre * squash * (1.0 + gate_pre * (1.0 - squash))
        up_by[:, cols] = swish
        hidden_t[cols, :] = (swish * up_pre).T.astype(BF16)


def part_columns(gate_grad, up_grad, gate_t, up_t, offset, own, other):
    rows, width = own.shape
    step = 256 if width % 256 == 0 else width
    for c in range(0, width, step):
        cols = slice(offset + c, offset + c + step)
        first = jnp.dot(gate_grad, gate_t[:, cols], preferred_element_type=F32)
        second = jnp.dot(up_grad, up_t[:, cols], preferred_element_type=F32)
        part = (first + second).astype(BF16)
        own[:, c : c + step] = part[:rows]
        other[:, c : c + step] = part[rows:]


def backward_kernel(n, width, *refs):
    pieces, refs = refs[:n], refs[n:]
    down_t, gate_t, up_t, gate_by, up_by, own, other, scaled, gate_grad, up_grad = refs
    expert = lax.axis_index("ep")
    start = 0
    for piece in pieces:
        spread = piece[:, width:].astype(F32)
        lane = lax.broadcasted_iota(jnp.int32, spread.shape, 1)
        weight = jnp.sum(jnp.where(lane == expert, spread, 0.0), axis=1, keepdims=True)
        rows = slice(start, start + piece.shape[0])
        scaled[rows, :] = (weight * piece[:, :width].astype(F32)).astype(BF16)
        start += piece.shape[0]
    hidden_grad = jnp.dot(scaled[...], down_t[...], preferred_element_type=F32)
    gates = (hidden_grad * gate_by[...]).astype(BF16)
    ups = (hidden_grad * up_by[...]).astype(BF16)
    gate_grad[...] = gates
    up_grad[...] = ups
    part_columns(gates, ups, gate_t, up_t, 0, own, other)


def backward(pieces, down_t, gate_t, up_t, gate_by, up_by):
    n = len(pieces)
    rows, units = gate_by.shape
    width = down_t.shape[0]
    half = jax.ShapeDtypeStruct((rows // 2, width // 2), BF16)
    return pl.pallas_call(
        functools.partial(backward_kernel, n, width),
        out_shape=(
            half,
            half,
            jax.ShapeDtypeStruct((rows, width), BF16),
            jax.ShapeDtypeStruct((rows, units), BF16),
            jax.ShapeDtypeStruct((rows, units), BF16),
        ),
        in_specs=[WHOLE] * (n + 5),
        out_specs=(WHOLE,) * 5,
        compiler_params=room(24),
        cost_estimate=QUICK,
        name="backward",
    )(*pieces, down_t, gate_t, up_t, gate_by, up_by)


def right_kernel(gate_grad, up_grad, gate_t, up_t, own, other):
    part_columns(gate_grad[...], up_grad[...], gate_t, up_t, own.shape[1], own, other)


def right_half(gate_grad, up_grad, gate_t, up_t):
    half = jax.ShapeDtypeStruct((gate_grad.shape[0] // 2, gate_t.shape[1] // 2), BF16)
    return pl.pallas_call(
        right_kernel,
        out_shape=(half, half),
        in_specs=[WHOLE] * 4,
        out_specs=(WHOLE,) * 2,
        compiler_params=room(16),
        cost_estimate=QUICK,
        name="right",
    )(gate_grad, up_grad, gate_t, up_t)


def outer_kernel(first, hidden_t, scaled, *refs):
    out, buffer, sem = refs[-3:]
    chunks, size = buffer.shape[:2]
    copies = []
    for n in range(chunks):
        rows = pl.ds((first * chunks + n) * size, size)
        buffer[n] = jnp.dot(hidden_t[rows, :], scaled[...], preferred_element_type=F32)
        copies.append(pltpu.make_async_copy(buffer.at[n], out.at[rows], sem.at[n]))
        copies[-1].start()
    for copy in copies:
        copy.wait()


def outer(first, hidden_t, scaled, *so_far):
    units, width = hidden_t.shape[0], scaled.shape[1]
    chunks = 4
    return pl.pallas_call(
        functools.partial(outer_kernel, first),
        out_shape=pltpu.HBM((units, width), F32),
        in_specs=[WHOLE] * 2 + [pl.BlockSpec(memory_space=pltpu.HBM)] * len(so_far),
        out_specs=pl.BlockSpec(memory_space=pltpu.HBM),
        scratch_shapes=[
            pltpu.VMEM((chunks, units // 2 // chunks, width), F32),
            pltpu.SemaphoreType.DMA((chunks,)),
        ],
        input_output_aliases={2: 0} if so_far else {},
        compiler_params=room(12),
        cost_estimate=QUICK,
        name="outer",
    )(hidden_t, scaled, *so_far)


def dense(activations, out_grad, route_weights, expert_ids, w_gate, w_up, w_down):
    n_ep = lax.axis_size("ep")
    n_sp = lax.axis_size("sp")
    tok_dev, width = activations.shape[1:]
    units = w_gate.shape[2]

    def swap(value, partner):
        return exchange(value, partner, n_sp, n_ep)

    far = [4 * j for j in range(1, n_ep // 4)][::-1]
    one = lambda i: i ^ n_ep if i & 1 else i ^ 2
    two = lambda i: i ^ 2 if i & 1 else i ^ n_ep
    core = lambda i: i ^ 1

    def gather(column):
        half = jnp.concatenate([column, swap(column, one)], axis=0)
        other = swap(half, core)
        rest = swap(half, two)
        return [half, rest, other, swap(rest, core)]

    mine = pack(activations, out_grad, route_weights, expert_ids, n_ep)
    blocks = {j: swap(mine, lambda i, j=j: i ^ j) for j in far}
    column_in, column_grad = stack([mine] + [blocks[j] for j in sorted(far)], width)
    rows_in = gather(column_in)
    rows_grad = gather(column_grad)
    gate_w, up_w = w_gate[0], w_up[0]
    gate_t, up_t = turn(gate_w, up_w)
    (down_t,) = turn(w_down[0])
    rows = sum(piece.shape[0] for piece in rows_in)
    n = len(rows_in)

    gate_by, up_by, hidden_t = pl.pallas_call(
        functools.partial(forward_kernel, n),
        out_shape=(
            jax.ShapeDtypeStruct((rows, units), F32),
            jax.ShapeDtypeStruct((rows, units), F32),
            jax.ShapeDtypeStruct((units, rows), BF16),
        ),
        in_specs=[WHOLE] * (n + 2),
        out_specs=(WHOLE,) * 3,
        compiler_params=room(16),
        cost_estimate=QUICK,
        name="forward",
    )(*rows_in, gate_w, up_w)
    own_left, other_left, scaled, gate_grad, up_grad = backward(
        rows_grad, down_t, gate_t, up_t, gate_by, up_by
    )
    own_right, other_right = right_half(gate_grad, up_grad, gate_t, up_t)
    owns = (own_left, own_right)
    got = [swap(x, core) for x in (other_left, other_right)]
    weight_grad = outer(0, hidden_t, scaled)
    weight_grad = outer(1, hidden_t, scaled, weight_grad)

    totals = [a.astype(F32) + b.astype(F32) for a, b in zip(owns, got)]
    for partner in (two, one):
        half = totals[0].shape[0] // 2
        got = [swap(x[half:].astype(BF16), partner) for x in totals]
        totals = [x[:half].astype(F32) + y.astype(F32) for x, y in zip(totals, got)]
    total = jnp.concatenate(totals, axis=1)
    sent = total.astype(BF16)
    own = total[:tok_dev]
    for j in back_order(far):
        block = sent[j // 4 * tok_dev : (j // 4 + 1) * tok_dev]
        own = own + swap(block, lambda i, j=j: i ^ j).astype(F32)
    return (own.astype(BF16)[None], weight_grad[None])


def per_device(activations, out_grad, route_weights, expert_ids, w_gate, w_up, w_down):
    n_ep = lax.axis_size("ep")
    n_sp = lax.axis_size("sp")
    tokens = activations.shape[1] * n_sp * n_ep
    rows = n_ep * max(2, activations.shape[1] * n_sp * TOP * 3 // (2 * n_ep))
    few = tokens <= 2 * rows and n_sp == 2 and n_ep >= 8 and n_ep & (n_ep - 1) == 0
    if not few:
        return routed(activations, out_grad, route_weights, expert_ids, w_gate, w_up, w_down)
    return dense(activations, out_grad, route_weights, expert_ids, w_gate, w_up, w_down)


def solution(mesh):
    return jax.shard_map(
        per_device,
        mesh=mesh,
        in_specs=(
            P("ep", "sp", None),
            P("ep", "sp", None),
            P("ep", "sp", None),
            P("ep", "sp", None),
            P("ep", None, "sp"),
            P("ep", None, "sp"),
            P("ep", "sp", None),
        ),
        out_specs=(P("ep", "sp", None), P("ep", "sp", None)),
        check_vma=False,
    )
```

```python
import functools

import jax
import jax.numpy as jnp
from jax import lax
from jax.experimental import pallas as pl
from jax.experimental.pallas import tpu as pltpu
from jax.sharding import PartitionSpec as P

TOP = 8
TURN = 512
F32 = jnp.float32
BF16 = jnp.bfloat16


def room(mib):
    return pltpu.CompilerParams(vmem_limit_bytes=mib * 2**20)


BUSY = pl.CostEstimate(flops=10**10, transcendentals=0, bytes_accessed=0)
QUICK = pl.CostEstimate(flops=10**6, transcendentals=0, bytes_accessed=0)
WHOLE = pl.BlockSpec(memory_space=pltpu.VMEM)


def expert_rows(rows_in, rows_grad, gate_w, up_w, down_w):
    gate_pre = jnp.dot(rows_in, gate_w, preferred_element_type=F32)
    up_pre = jnp.dot(rows_in, up_w, preferred_element_type=F32)
    squash = jax.nn.sigmoid(gate_pre)
    swish = gate_pre * squash
    hidden = (swish * up_pre).astype(BF16)
    hidden_grad = lax.dot_general(
        rows_grad, down_w, (((1,), (1,)), ((), ())), preferred_element_type=F32
    )
    gate_grad = (hidden_grad * up_pre * squash * (1.0 + gate_pre * (1.0 - squash))).astype(BF16)
    up_grad = (hidden_grad * swish).astype(BF16)
    first = lax.dot_general(
        gate_grad, gate_w, (((1,), (1,)), ((), ())), preferred_element_type=F32
    )
    second = lax.dot_general(up_grad, up_w, (((1,), (1,)), ((), ())), preferred_element_type=F32)
    partial_rows = (first + second).astype(BF16)
    weight_grad = lax.dot_general(
        hidden, rows_grad, (((0,), (0,)), ((), ())), preferred_element_type=F32
    )
    return (partial_rows, weight_grad)


def routed(activations, out_grad, route_weights, expert_ids, w_gate, w_up, w_down):
    n_expert = lax.axis_size("ep")
    n_group = lax.axis_size("sp")
    tok_dev = activations.shape[1]
    width = activations.shape[2]
    capacity = max(2, tok_dev * n_group * TOP * 3 // (2 * n_expert))
    group_ids = lax.all_gather(expert_ids, "sp", axis=1, tiled=True)
    group_in, group_grad, group_weight = (
        lax.all_gather(activations, "sp", axis=1, tiled=True),
        lax.all_gather(out_grad, "sp", axis=1, tiled=True),
        lax.all_gather(route_weights, "sp", axis=1, tiled=True),
    )
    tok_grp = group_ids.shape[1]
    slot_expert = group_ids[0].reshape(-1)
    slot_token = jnp.arange(slot_expert.shape[0], dtype=jnp.int32) // TOP
    onehot = (slot_expert[:, None] == jnp.arange(n_expert, dtype=jnp.int32)[None, :]).astype(
        jnp.int32
    )
    before = jnp.cumsum(onehot, axis=0) - onehot
    rank = jnp.sum(before * onehot, axis=1)
    position = slot_expert * capacity + rank
    total_rows = n_expert * capacity
    token_in = group_in[0][slot_token]
    scaled = (
        group_weight[0].reshape(-1).astype(F32)[:, None] * group_grad[0][slot_token].astype(F32)
    ).astype(BF16)
    send_in = (
        jnp.zeros((total_rows, width), BF16)
        .at[position]
        .set(token_in)
        .reshape(n_expert, capacity, width)
    )
    send_grad = (
        jnp.zeros((total_rows, width), BF16)
        .at[position]
        .set(scaled)
        .reshape(n_expert, capacity, width)
    )
    recv_in, recv_grad = (
        lax.all_to_all(send_in, "ep", split_axis=0, concat_axis=0, tiled=True),
        lax.all_to_all(send_grad, "ep", split_axis=0, concat_axis=0, tiled=True),
    )
    flat_in = recv_in.reshape(total_rows, width)
    flat_grad = recv_grad.reshape(total_rows, width)
    partial_rows, weight_grad = expert_rows(flat_in, flat_grad, w_gate[0], w_up[0], w_down[0])
    partial_rows = partial_rows.reshape(n_expert, capacity, width)
    slot_owner = jnp.full((total_rows,), -1, jnp.int32).at[position].set(slot_token)
    owner_match = jnp.arange(tok_grp, dtype=jnp.int32)[:, None] == slot_owner[None, :]
    back_rows = lax.all_to_all(partial_rows, "ep", split_axis=0, concat_axis=0, tiled=True)
    token_sum = jnp.dot(
        owner_match.astype(BF16),
        back_rows.reshape(total_rows, width),
        preferred_element_type=F32,
    )
    own_sum = lax.psum_scatter(token_sum.astype(BF16), "sp", scatter_dimension=0, tiled=True)
    return (own_sum.reshape(1, tok_dev, width), weight_grad[None])


def back_order(far):
    return far[:1] + far[-1:] + far[1:-1] if len(far) > 1 else far


def exchange(value, partner, n_sp, n_ep):
    pairs = [(i, partner(i)) for i in range(n_sp * n_ep)]
    return lax.ppermute(value, ("sp", "ep"), pairs)


def pack_kernel(in_ref, grad_ref, weight_ref, ids_ref, out_ref, rows, weights, ids, sem):
    tok_dev, width = in_ref.shape[1:]
    copies = [
        pltpu.make_async_copy(source, target, sem.at[n])
        for n, (source, target) in enumerate(
            (
                (weight_ref, weights),
                (ids_ref, ids),
                (in_ref.at[0], rows.at[0]),
                (grad_ref.at[0], rows.at[1]),
            )
        )
    ]
    for copy in copies:
        copy.start()
    for copy in copies:
        copy.wait()
    lane = lax.broadcasted_iota(jnp.int32, (tok_dev, out_ref.shape[1] - width), 1)
    weight = weights[0].astype(F32)
    spread = jnp.zeros(lane.shape, F32)
    for k in range(ids.shape[2]):
        spread += jnp.where(lane == ids[0, :, k : k + 1], weight[:, k : k + 1], 0.0)
    out_ref[:tok_dev, :width] = rows[0]
    out_ref[:tok_dev, width:] = jnp.zeros(lane.shape, BF16)
    out_ref[tok_dev:, :width] = rows[1]
    out_ref[tok_dev:, width:] = spread.astype(BF16)


def pack(activations, out_grad, route_weights, expert_ids, n_expert):
    _, tok_dev, width = out_grad.shape
    operands = (activations, out_grad, route_weights, expert_ids)
    return pl.pallas_call(
        pack_kernel,
        out_shape=jax.ShapeDtypeStruct((2 * tok_dev, width + n_expert + -n_expert % 128), BF16),
        in_specs=[pl.BlockSpec(memory_space=pltpu.HBM)] * 4,
        out_specs=WHOLE,
        scratch_shapes=[
            pltpu.VMEM((2, tok_dev, width), BF16),
            pltpu.VMEM(route_weights.shape, route_weights.dtype),
            pltpu.VMEM(expert_ids.shape, expert_ids.dtype),
            pltpu.SemaphoreType.DMA((4,)),
        ],
        compiler_params=room(2),
        cost_estimate=BUSY,
        name="pack",
    )(*(pltpu.with_memory_space_constraint(x, pltpu.HBM) for x in operands))


def split_kernel(*refs):
    in_ref, grad_ref = refs[-2:]
    _, rows, width = in_ref.shape
    for n, ref in enumerate(refs[:-2]):
        in_ref[n] = ref[:rows, :width]
        grad_ref[n] = ref[rows:, :]


def split(blocks, width):
    rows, wide = blocks[0].shape
    n, rows = len(blocks), rows // 2
    return pl.pallas_call(
        split_kernel,
        out_shape=(
            jax.ShapeDtypeStruct((n, rows, width), BF16),
            jax.ShapeDtypeStruct((n, rows, wide), BF16),
        ),
        in_specs=[WHOLE] * n,
        out_specs=(WHOLE,) * 2,
        compiler_params=room(2),
        cost_estimate=QUICK,
        name="split",
    )(*blocks)


def place(near, away, skip, rows):
    tok_dev, width = away[0].shape[1], rows.shape[1]
    start = 0
    for block, others in zip(near, away):
        pack_rows = block.shape[0] // 2
        per = others.shape[0] // 2
        for p in range(2):
            first = p * pack_rows + skip
            rows[start : start + tok_dev, :] = block[first : first + tok_dev, :width]
            start += tok_dev
            for n in range(per):
                rows[start : start + tok_dev, :] = others[p * per + n]
                start += tok_dev


def lay_kernel(n, *refs):
    place(refs[:n], refs[n : 2 * n], 0, refs[2 * n])


def lay(near, away, rows):
    n = len(near)
    return pl.pallas_call(
        functools.partial(lay_kernel, n),
        out_shape=jax.ShapeDtypeStruct((rows, away[0].shape[2]), BF16),
        in_specs=[WHOLE] * (2 * n),
        out_specs=WHOLE,
        compiler_params=room(4),
        cost_estimate=QUICK,
        name="lay",
    )(*near, *away)


def turn_kernel(n, *refs):
    for source, target in zip(refs[:n], refs[n:]):
        for c in range(0, source.shape[0], TURN):
            rows = slice(c, min(c + TURN, source.shape[0]))
            target[:, rows] = source[rows, :].T


def turn(*weights):
    n = len(weights)
    return pl.pallas_call(
        functools.partial(turn_kernel, n),
        out_shape=[jax.ShapeDtypeStruct(w.shape[::-1], w.dtype) for w in weights],
        in_specs=[WHOLE] * n,
        out_specs=[WHOLE] * n,
        compiler_params=room(16),
        cost_estimate=QUICK,
        name="turn",
    )(*weights)


def forward_kernel(rows, gate_w, up_w, gate_by, up_by, hidden_t):
    step = min(256, gate_w.shape[1])
    for c in range(0, gate_w.shape[1], step):
        cols = slice(c, c + step)
        gate_pre = jnp.dot(rows[...], gate_w[:, cols], preferred_element_type=F32)
        up_pre = jnp.dot(rows[...], up_w[:, cols], preferred_element_type=F32)
        squash = jax.nn.sigmoid(gate_pre)
        swish = gate_pre * squash
        gate_by[:, cols] = up_pre * squash * (1.0 + gate_pre * (1.0 - squash))
        up_by[:, cols] = swish
        hidden_t[cols, :] = (swish * up_pre).T.astype(BF16)


def part_columns(gate_grad, up_grad, gate_t, up_t, offset, own, other):
    rows, width = own.shape
    step = 256 if width % 256 == 0 else width
    for c in range(0, width, step):
        cols = slice(offset + c, offset + c + step)
        first = jnp.dot(gate_grad, gate_t[:, cols], preferred_element_type=F32)
        second = jnp.dot(up_grad, up_t[:, cols], preferred_element_type=F32)
        part = (first + second).astype(BF16)
        own[:, c : c + step] = part[:rows]
        other[:, c : c + step] = part[rows:]


def backward_kernel(n, width, *refs):
    near, away, refs = refs[:n], refs[n : 2 * n], refs[2 * n :]
    down_t, gate_t, up_t, gate_by, up_by, own, other, scaled, gate_grad, up_grad, placed = refs
    place(near, away, away[0].shape[1], placed)
    expert = lax.axis_index("ep")
    spread = placed[:, width:].astype(F32)
    lane = lax.broadcasted_iota(jnp.int32, spread.shape, 1)
    weight = jnp.sum(jnp.where(lane == expert, spread, 0.0), axis=1, keepdims=True)
    scaled[...] = (weight * placed[:, :width].astype(F32)).astype(BF16)
    hidden_grad = jnp.dot(scaled[...], down_t[...], preferred_element_type=F32)
    gates = (hidden_grad * gate_by[...]).astype(BF16)
    ups = (hidden_grad * up_by[...]).astype(BF16)
    gate_grad[...] = gates
    up_grad[...] = ups
    part_columns(gates, ups, gate_t, up_t, 0, own, other)


def backward(near, away, down_t, gate_t, up_t, gate_by, up_by):
    n = len(near)
    rows, units = gate_by.shape
    width = down_t.shape[0]
    half = jax.ShapeDtypeStruct((rows // 2, width // 2), BF16)
    return pl.pallas_call(
        functools.partial(backward_kernel, n, width),
        out_shape=(
            half,
            half,
            jax.ShapeDtypeStruct((rows, width), BF16),
            jax.ShapeDtypeStruct((rows, units), BF16),
            jax.ShapeDtypeStruct((rows, units), BF16),
        ),
        in_specs=[WHOLE] * (2 * n + 5),
        out_specs=(WHOLE,) * 5,
        scratch_shapes=[pltpu.VMEM((rows, away[0].shape[2]), BF16)],
        compiler_params=room(24),
        cost_estimate=QUICK,
        name="backward",
    )(*near, *away, down_t, gate_t, up_t, gate_by, up_by)


def right_kernel(gate_grad, up_grad, gate_t, up_t, own, other):
    part_columns(gate_grad[...], up_grad[...], gate_t, up_t, own.shape[1], own, other)


def right_half(gate_grad, up_grad, gate_t, up_t):
    half = jax.ShapeDtypeStruct((gate_grad.shape[0] // 2, gate_t.shape[1] // 2), BF16)
    return pl.pallas_call(
        right_kernel,
        out_shape=(half, half),
        in_specs=[WHOLE] * 4,
        out_specs=(WHOLE,) * 2,
        compiler_params=room(16),
        cost_estimate=QUICK,
        name="right",
    )(gate_grad, up_grad, gate_t, up_t)


def outer_kernel(first, hidden_t, scaled, *refs):
    out, buffer, sem = refs[-3:]
    chunks, size = buffer.shape[:2]
    copies = []
    for n in range(chunks):
        rows = pl.ds((first * chunks + n) * size, size)
        buffer[n] = jnp.dot(hidden_t[rows, :], scaled[...], preferred_element_type=F32)
        copies.append(pltpu.make_async_copy(buffer.at[n], out.at[rows], sem.at[n]))
        copies[-1].start()
    for copy in copies:
        copy.wait()


def outer(first, hidden_t, scaled, *so_far):
    units, width = hidden_t.shape[0], scaled.shape[1]
    chunks = 4
    return pl.pallas_call(
        functools.partial(outer_kernel, first),
        out_shape=pltpu.HBM((units, width), F32),
        in_specs=[WHOLE] * 2 + [pl.BlockSpec(memory_space=pltpu.HBM)] * len(so_far),
        out_specs=pl.BlockSpec(memory_space=pltpu.HBM),
        scratch_shapes=[
            pltpu.VMEM((chunks, units // 2 // chunks, width), F32),
            pltpu.SemaphoreType.DMA((chunks,)),
        ],
        input_output_aliases={2: 0} if so_far else {},
        compiler_params=room(12),
        cost_estimate=QUICK,
        name="outer",
    )(hidden_t, scaled, *so_far)


def dense(activations, out_grad, route_weights, expert_ids, w_gate, w_up, w_down):
    n_ep = lax.axis_size("ep")
    n_sp = lax.axis_size("sp")
    tok_dev, width = activations.shape[1:]
    units = w_gate.shape[2]

    def swap(value, partner):
        return exchange(value, partner, n_sp, n_ep)

    far = [4 * j for j in range(1, n_ep // 4)][::-1]
    one = lambda i: i ^ n_ep if i & 1 else i ^ 2
    two = lambda i: i ^ 2 if i & 1 else i ^ n_ep
    core = lambda i: i ^ 1

    def gather(column):
        half = jnp.concatenate([column, swap(column, one)], axis=0)
        other = swap(half, core)
        rest = swap(half, two)
        return [half, rest, other, swap(rest, core)]

    mine = pack(activations, out_grad, route_weights, expert_ids, n_ep)
    blocks = {j: swap(mine, lambda i, j=j: i ^ j) for j in far}
    near = gather(mine)
    far_in, far_grad = split([blocks[j] for j in sorted(far)], width)
    rows_in = gather(far_in)
    rows_grad = gather(far_grad)
    gate_w, up_w = w_gate[0], w_up[0]
    gate_t, up_t = turn(gate_w, up_w)
    (down_t,) = turn(w_down[0])
    rows = tok_dev * n_ep * n_sp
    placed = lay(near, rows_in, rows)

    gate_by, up_by, hidden_t = pl.pallas_call(
        forward_kernel,
        out_shape=(
            jax.ShapeDtypeStruct((rows, units), F32),
            jax.ShapeDtypeStruct((rows, units), F32),
            jax.ShapeDtypeStruct((units, rows), BF16),
        ),
        in_specs=[WHOLE] * 3,
        out_specs=(WHOLE,) * 3,
        compiler_params=room(16),
        cost_estimate=QUICK,
        name="forward",
    )(placed, gate_w, up_w)
    own_left, other_left, scaled, gate_grad, up_grad = backward(
        near, rows_grad, down_t, gate_t, up_t, gate_by, up_by
    )
    own_right, other_right = right_half(gate_grad, up_grad, gate_t, up_t)
    owns = (own_left, own_right)
    got = [swap(x, core) for x in (other_left, other_right)]
    weight_grad = outer(0, hidden_t, scaled)
    weight_grad = outer(1, hidden_t, scaled, weight_grad)

    totals = [a.astype(F32) + b.astype(F32) for a, b in zip(owns, got)]
    for partner in (two, one):
        half = totals[0].shape[0] // 2
        got = [swap(x[half:].astype(BF16), partner) for x in totals]
        totals = [x[:half].astype(F32) + y.astype(F32) for x, y in zip(totals, got)]
    total = jnp.concatenate(totals, axis=1)
    sent = total.astype(BF16)
    own = total[:tok_dev]
    for j in back_order(far):
        block = sent[j // 4 * tok_dev : (j // 4 + 1) * tok_dev]
        own = own + swap(block, lambda i, j=j: i ^ j).astype(F32)
    return (own.astype(BF16)[None], weight_grad[None])


def per_device(activations, out_grad, route_weights, expert_ids, w_gate, w_up, w_down):
    n_ep = lax.axis_size("ep")
    n_sp = lax.axis_size("sp")
    tokens = activations.shape[1] * n_sp * n_ep
    rows = n_ep * max(2, activations.shape[1] * n_sp * TOP * 3 // (2 * n_ep))
    few = tokens <= 2 * rows and n_sp == 2 and n_ep >= 8 and n_ep & (n_ep - 1) == 0
    if not few:
        return routed(activations, out_grad, route_weights, expert_ids, w_gate, w_up, w_down)
    return dense(activations, out_grad, route_weights, expert_ids, w_gate, w_up, w_down)


def solution(mesh):
    return jax.shard_map(
        per_device,
        mesh=mesh,
        in_specs=(
            P("ep", "sp", None),
            P("ep", "sp", None),
            P("ep", "sp", None),
            P("ep", "sp", None),
            P("ep", None, "sp"),
            P("ep", None, "sp"),
            P("ep", "sp", None),
        ),
        out_specs=(P("ep", "sp", None), P("ep", "sp", None)),
        check_vma=False,
    )
```

```python
import functools

import jax
import jax.numpy as jnp
from jax import lax
from jax.experimental import pallas as pl
from jax.experimental.pallas import tpu as pltpu
from jax.sharding import PartitionSpec as P

TOP = 8
TURN = 512
F32 = jnp.float32
BF16 = jnp.bfloat16


def room(mib):
    return pltpu.CompilerParams(vmem_limit_bytes=mib * 2**20)


BUSY = pl.CostEstimate(flops=10**10, transcendentals=0, bytes_accessed=0)
QUICK = pl.CostEstimate(flops=10**6, transcendentals=0, bytes_accessed=0)
WHOLE = pl.BlockSpec(memory_space=pltpu.VMEM)


def expert_rows(rows_in, rows_grad, gate_w, up_w, down_w):
    gate_pre = jnp.dot(rows_in, gate_w, preferred_element_type=F32)
    up_pre = jnp.dot(rows_in, up_w, preferred_element_type=F32)
    squash = jax.nn.sigmoid(gate_pre)
    swish = gate_pre * squash
    hidden = (swish * up_pre).astype(BF16)
    hidden_grad = lax.dot_general(
        rows_grad, down_w, (((1,), (1,)), ((), ())), preferred_element_type=F32
    )
    gate_grad = (hidden_grad * up_pre * squash * (1.0 + gate_pre * (1.0 - squash))).astype(BF16)
    up_grad = (hidden_grad * swish).astype(BF16)
    first = lax.dot_general(
        gate_grad, gate_w, (((1,), (1,)), ((), ())), preferred_element_type=F32
    )
    second = lax.dot_general(up_grad, up_w, (((1,), (1,)), ((), ())), preferred_element_type=F32)
    partial_rows = (first + second).astype(BF16)
    weight_grad = lax.dot_general(
        hidden, rows_grad, (((0,), (0,)), ((), ())), preferred_element_type=F32
    )
    return (partial_rows, weight_grad)


def routed(activations, out_grad, route_weights, expert_ids, w_gate, w_up, w_down):
    n_expert = lax.axis_size("ep")
    n_group = lax.axis_size("sp")
    tok_dev = activations.shape[1]
    width = activations.shape[2]
    capacity = max(2, tok_dev * n_group * TOP * 3 // (2 * n_expert))
    group_ids = lax.all_gather(expert_ids, "sp", axis=1, tiled=True)
    group_in, group_grad, group_weight = (
        lax.all_gather(activations, "sp", axis=1, tiled=True),
        lax.all_gather(out_grad, "sp", axis=1, tiled=True),
        lax.all_gather(route_weights, "sp", axis=1, tiled=True),
    )
    tok_grp = group_ids.shape[1]
    slot_expert = group_ids[0].reshape(-1)
    slot_token = jnp.arange(slot_expert.shape[0], dtype=jnp.int32) // TOP
    onehot = (slot_expert[:, None] == jnp.arange(n_expert, dtype=jnp.int32)[None, :]).astype(
        jnp.int32
    )
    before = jnp.cumsum(onehot, axis=0) - onehot
    rank = jnp.sum(before * onehot, axis=1)
    position = slot_expert * capacity + rank
    total_rows = n_expert * capacity
    token_in = group_in[0][slot_token]
    scaled = (
        group_weight[0].reshape(-1).astype(F32)[:, None] * group_grad[0][slot_token].astype(F32)
    ).astype(BF16)
    send_in = (
        jnp.zeros((total_rows, width), BF16)
        .at[position]
        .set(token_in)
        .reshape(n_expert, capacity, width)
    )
    send_grad = (
        jnp.zeros((total_rows, width), BF16)
        .at[position]
        .set(scaled)
        .reshape(n_expert, capacity, width)
    )
    recv_in, recv_grad = (
        lax.all_to_all(send_in, "ep", split_axis=0, concat_axis=0, tiled=True),
        lax.all_to_all(send_grad, "ep", split_axis=0, concat_axis=0, tiled=True),
    )
    flat_in = recv_in.reshape(total_rows, width)
    flat_grad = recv_grad.reshape(total_rows, width)
    partial_rows, weight_grad = expert_rows(flat_in, flat_grad, w_gate[0], w_up[0], w_down[0])
    partial_rows = partial_rows.reshape(n_expert, capacity, width)
    slot_owner = jnp.full((total_rows,), -1, jnp.int32).at[position].set(slot_token)
    owner_match = jnp.arange(tok_grp, dtype=jnp.int32)[:, None] == slot_owner[None, :]
    back_rows = lax.all_to_all(partial_rows, "ep", split_axis=0, concat_axis=0, tiled=True)
    token_sum = jnp.dot(
        owner_match.astype(BF16),
        back_rows.reshape(total_rows, width),
        preferred_element_type=F32,
    )
    own_sum = lax.psum_scatter(token_sum.astype(BF16), "sp", scatter_dimension=0, tiled=True)
    return (own_sum.reshape(1, tok_dev, width), weight_grad[None])


def back_order(far):
    return far[:1] + far[-1:] + far[1:-1] if len(far) > 1 else far


def exchange(value, partner, n_sp, n_ep):
    pairs = [(i, partner(i)) for i in range(n_sp * n_ep)]
    return lax.ppermute(value, ("sp", "ep"), pairs)


def pack_kernel(in_ref, grad_ref, weight_ref, ids_ref, out_ref, rows, weights, ids, sem):
    tok_dev, width = in_ref.shape[1:]
    copies = [
        pltpu.make_async_copy(source, target, sem.at[n])
        for n, (source, target) in enumerate(
            (
                (weight_ref, weights),
                (ids_ref, ids),
                (in_ref.at[0], rows.at[0]),
                (grad_ref.at[0], rows.at[1]),
            )
        )
    ]
    for copy in copies:
        copy.start()
    for copy in copies:
        copy.wait()
    lane = lax.broadcasted_iota(jnp.int32, (tok_dev, out_ref.shape[1] - width), 1)
    weight = weights[0].astype(F32)
    spread = jnp.zeros(lane.shape, F32)
    for k in range(ids.shape[2]):
        spread += jnp.where(lane == ids[0, :, k : k + 1], weight[:, k : k + 1], 0.0)
    out_ref[:tok_dev, :width] = rows[0]
    out_ref[:tok_dev, width:] = jnp.zeros(lane.shape, BF16)
    out_ref[tok_dev:, :width] = rows[1]
    out_ref[tok_dev:, width:] = spread.astype(BF16)


def pack(activations, out_grad, route_weights, expert_ids, n_expert):
    _, tok_dev, width = out_grad.shape
    operands = (activations, out_grad, route_weights, expert_ids)
    return pl.pallas_call(
        pack_kernel,
        out_shape=jax.ShapeDtypeStruct((2 * tok_dev, width + n_expert + -n_expert % 128), BF16),
        in_specs=[pl.BlockSpec(memory_space=pltpu.HBM)] * 4,
        out_specs=WHOLE,
        scratch_shapes=[
            pltpu.VMEM((2, tok_dev, width), BF16),
            pltpu.VMEM(route_weights.shape, route_weights.dtype),
            pltpu.VMEM(expert_ids.shape, expert_ids.dtype),
            pltpu.SemaphoreType.DMA((4,)),
        ],
        compiler_params=room(2),
        cost_estimate=BUSY,
        name="pack",
    )(*(pltpu.with_memory_space_constraint(x, pltpu.HBM) for x in operands))


def split_kernel(*refs):
    in_ref, grad_ref = refs[-2:]
    _, rows, width = in_ref.shape
    for n, ref in enumerate(refs[:-2]):
        in_ref[n] = ref[:rows, :width]
        grad_ref[n] = ref[rows:, :]


def split(blocks, width):
    rows, wide = blocks[0].shape
    n, rows = len(blocks), rows // 2
    return pl.pallas_call(
        split_kernel,
        out_shape=(
            jax.ShapeDtypeStruct((n, rows, width), BF16),
            jax.ShapeDtypeStruct((n, rows, wide), BF16),
        ),
        in_specs=[WHOLE] * n,
        out_specs=(WHOLE,) * 2,
        compiler_params=room(2),
        cost_estimate=QUICK,
        name="split",
    )(*blocks)


def place(near, away, skip, rows):
    tok_dev, width = away[0].shape[1], rows.shape[1]
    start = 0
    for block, others in zip(near, away):
        pack_rows = block.shape[0] // 2
        per = others.shape[0] // 2
        for p in range(2):
            first = p * pack_rows + skip
            rows[start : start + tok_dev, :] = block[first : first + tok_dev, :width]
            start += tok_dev
            for n in range(per):
                rows[start : start + tok_dev, :] = others[p * per + n]
                start += tok_dev


def lay_kernel(n, *refs):
    place(refs[:n], refs[n : 2 * n], 0, refs[2 * n])


def lay(near, away, rows):
    n = len(near)
    return pl.pallas_call(
        functools.partial(lay_kernel, n),
        out_shape=jax.ShapeDtypeStruct((rows, away[0].shape[2]), BF16),
        in_specs=[WHOLE] * (2 * n),
        out_specs=WHOLE,
        compiler_params=room(4),
        cost_estimate=QUICK,
        name="lay",
    )(*near, *away)


def turn_kernel(n, *refs):
    for source, target in zip(refs[:n], refs[n:]):
        for c in range(0, source.shape[0], TURN):
            rows = slice(c, min(c + TURN, source.shape[0]))
            target[:, rows] = source[rows, :].T


def turn(*weights):
    n = len(weights)
    return pl.pallas_call(
        functools.partial(turn_kernel, n),
        out_shape=[jax.ShapeDtypeStruct(w.shape[::-1], w.dtype) for w in weights],
        in_specs=[WHOLE] * n,
        out_specs=[WHOLE] * n,
        compiler_params=room(16),
        cost_estimate=QUICK,
        name="turn",
    )(*weights)


def forward_kernel(rows, gate_w, up_w, gate_by, up_by, hidden_t):
    step = min(256, gate_w.shape[1])
    for c in range(0, gate_w.shape[1], step):
        cols = slice(c, c + step)
        gate_pre = jnp.dot(rows[...], gate_w[:, cols], preferred_element_type=F32)
        up_pre = jnp.dot(rows[...], up_w[:, cols], preferred_element_type=F32)
        squash = jax.nn.sigmoid(gate_pre)
        swish = gate_pre * squash
        gate_by[:, cols] = up_pre * squash * (1.0 + gate_pre * (1.0 - squash))
        up_by[:, cols] = swish
        hidden_t[cols, :] = (swish * up_pre).T.astype(BF16)


def backward_kernel(n, width, *refs):
    near, away, refs = refs[:n], refs[n : 2 * n], refs[2 * n :]
    down_t, gate_t, up_t, gate_by, up_by, scaled, own, *others, placed = refs
    place(near, away, away[0].shape[1], placed)
    expert = lax.axis_index("ep")
    spread = placed[:, width:].astype(F32)
    lane = lax.broadcasted_iota(jnp.int32, spread.shape, 1)
    weight = jnp.sum(jnp.where(lane == expert, spread, 0.0), axis=1, keepdims=True)
    scaled[...] = (weight * placed[:, :width].astype(F32)).astype(BF16)
    hidden_grad = jnp.dot(scaled[...], down_t[...], preferred_element_type=F32)
    gate_grad = (hidden_grad * gate_by[...]).astype(BF16)
    up_grad = (hidden_grad * up_by[...]).astype(BF16)
    kept = own.shape[0]
    step = 256 if width % 256 == 0 else width
    for c in range(0, width, step):
        cols = slice(c, c + step)
        first = jnp.dot(gate_grad, gate_t[:, cols], preferred_element_type=F32)
        second = jnp.dot(up_grad, up_t[:, cols], preferred_element_type=F32)
        part = (first + second).astype(BF16)
        own[:, cols] = part[:kept]
        start = kept
        for other in others:
            other[:, cols] = part[start : start + other.shape[0]]
            start += other.shape[0]


def backward(near, away, down_t, gate_t, up_t, gate_by, up_by):
    n = len(near)
    rows = gate_by.shape[0]
    width = down_t.shape[0]
    return pl.pallas_call(
        functools.partial(backward_kernel, n, width),
        out_shape=(
            jax.ShapeDtypeStruct((rows, width), BF16),
            jax.ShapeDtypeStruct((rows // 2, width), BF16),
            jax.ShapeDtypeStruct((rows * 3 // 8, width), BF16),
            jax.ShapeDtypeStruct((rows // 8, width), BF16),
        ),
        in_specs=[WHOLE] * (2 * n + 5),
        out_specs=(WHOLE,) * 4,
        scratch_shapes=[pltpu.VMEM((rows, away[0].shape[2]), BF16)],
        compiler_params=room(24),
        cost_estimate=QUICK,
        name="backward",
    )(*near, *away, down_t, gate_t, up_t, gate_by, up_by)


def outer_kernel(start, hidden_t, scaled, *refs):
    out, buffer, sem = refs[-3:]
    chunks, size = buffer.shape[:2]
    copies = []
    for n in range(chunks):
        rows = pl.ds(start + n * size, size)
        buffer[n] = jnp.dot(hidden_t[rows, :], scaled[...], preferred_element_type=F32)
        copies.append(pltpu.make_async_copy(buffer.at[n], out.at[rows], sem.at[n]))
        copies[-1].start()
    for copy in copies:
        copy.wait()


def outer(start, chunks, hidden_t, scaled, *so_far):
    units, width = hidden_t.shape[0], scaled.shape[1]
    return pl.pallas_call(
        functools.partial(outer_kernel, start * (units // 8)),
        out_shape=pltpu.HBM((units, width), F32),
        in_specs=[WHOLE] * 2 + [pl.BlockSpec(memory_space=pltpu.HBM)] * len(so_far),
        out_specs=pl.BlockSpec(memory_space=pltpu.HBM),
        scratch_shapes=[
            pltpu.VMEM((chunks, units // 8, width), F32),
            pltpu.SemaphoreType.DMA((chunks,)),
        ],
        input_output_aliases={2: 0} if so_far else {},
        compiler_params=room(12),
        cost_estimate=QUICK,
        name="outer",
    )(hidden_t, scaled, *so_far)


def add_kernel(starts, *refs):
    out = refs[-1]
    rows = out.shape[0]
    total = sum(ref[n : n + rows, :].astype(F32) for n, ref in zip(starts, refs))
    out[...] = total.astype(BF16)


def add_rows(rows, *terms):
    return pl.pallas_call(
        functools.partial(add_kernel, [start for _, start in terms]),
        out_shape=jax.ShapeDtypeStruct((rows, terms[0][0].shape[1]), BF16),
        in_specs=[WHOLE] * len(terms),
        out_specs=WHOLE,
        compiler_params=room(4),
        cost_estimate=QUICK,
        name="add",
    )(*(array for array, _ in terms))


def dense(activations, out_grad, route_weights, expert_ids, w_gate, w_up, w_down):
    n_ep = lax.axis_size("ep")
    n_sp = lax.axis_size("sp")
    tok_dev, width = activations.shape[1:]
    units = w_gate.shape[2]

    def swap(value, partner):
        return exchange(value, partner, n_sp, n_ep)

    far = [4 * j for j in range(1, n_ep // 4)][::-1]
    one = lambda i: i ^ n_ep if i & 1 else i ^ 2
    two = lambda i: i ^ 2 if i & 1 else i ^ n_ep
    core = lambda i: i ^ 1

    def gather(column):
        half = jnp.concatenate([column, swap(column, one)], axis=0)
        other = swap(half, core)
        rest = swap(half, two)
        return [half, rest, other, swap(rest, core)]

    mine = pack(activations, out_grad, route_weights, expert_ids, n_ep)
    blocks = {j: swap(mine, lambda i, j=j: i ^ j) for j in far}
    near = gather(mine)
    far_in, far_grad = split([blocks[j] for j in sorted(far)], width)
    rows_in = gather(far_in)
    rows_grad = gather(far_grad)
    gate_w, up_w = w_gate[0], w_up[0]
    gate_t, up_t = turn(gate_w, up_w)
    (down_t,) = turn(w_down[0])
    rows = tok_dev * n_ep * n_sp
    placed = lay(near, rows_in, rows)

    gate_by, up_by, hidden_t = pl.pallas_call(
        forward_kernel,
        out_shape=(
            jax.ShapeDtypeStruct((rows, units), F32),
            jax.ShapeDtypeStruct((rows, units), F32),
            jax.ShapeDtypeStruct((units, rows), BF16),
        ),
        in_specs=[WHOLE] * 3,
        out_specs=(WHOLE,) * 3,
        compiler_params=room(16),
        cost_estimate=QUICK,
        name="forward",
    )(placed, gate_w, up_w)
    scaled, kept, other, other_corner = backward(
        near, rows_grad, down_t, gate_t, up_t, gate_by, up_by
    )
    weight_grad = ()
    for start, chunks in ((0, 2), (2, 2), (4, 4)):
        weight_grad = (outer(start, chunks, hidden_t, scaled, *weight_grad),)
    weight_grad = weight_grad[0]

    size = kept.shape[0] // 4
    got = swap(other_corner, core)
    corner = add_rows(size, (kept, 3 * size), (got, 0))
    passed = swap(corner, two)
    got = swap(other, core)
    second = add_rows(size, (kept, 2 * size), (got, 2 * size))
    second = swap(second, two)
    first = add_rows(size, (kept, size), (got, size), (passed, 0))
    first = swap(first, one)
    total = kept[:size].astype(F32) + got[:size].astype(F32)
    total = total + second.astype(F32) + first.astype(F32)
    sent = total.astype(BF16)
    own = total[:tok_dev]
    for j in back_order(far):
        block = sent[j // 4 * tok_dev : (j // 4 + 1) * tok_dev]
        own = own + swap(block, lambda i, j=j: i ^ j).astype(F32)
    return (own.astype(BF16)[None], weight_grad[None])


def per_device(activations, out_grad, route_weights, expert_ids, w_gate, w_up, w_down):
    n_ep = lax.axis_size("ep")
    n_sp = lax.axis_size("sp")
    tokens = activations.shape[1] * n_sp * n_ep
    rows = n_ep * max(2, activations.shape[1] * n_sp * TOP * 3 // (2 * n_ep))
    few = tokens <= 2 * rows and n_sp == 2 and n_ep >= 8 and n_ep & (n_ep - 1) == 0
    if not few:
        return routed(activations, out_grad, route_weights, expert_ids, w_gate, w_up, w_down)
    return dense(activations, out_grad, route_weights, expert_ids, w_gate, w_up, w_down)


def solution(mesh):
    return jax.shard_map(
        per_device,
        mesh=mesh,
        in_specs=(
            P("ep", "sp", None),
            P("ep", "sp", None),
            P("ep", "sp", None),
            P("ep", "sp", None),
            P("ep", None, "sp"),
            P("ep", None, "sp"),
            P("ep", "sp", None),
        ),
        out_specs=(P("ep", "sp", None), P("ep", "sp", None)),
        check_vma=False,
    )
```

```python
import functools

import jax
import jax.numpy as jnp
from jax import lax
from jax.experimental import pallas as pl
from jax.experimental.pallas import tpu as pltpu
from jax.sharding import PartitionSpec as P

TOP = 8
TURN = 512
F32 = jnp.float32
BF16 = jnp.bfloat16


def room(mib):
    return pltpu.CompilerParams(vmem_limit_bytes=mib * 2**20)


BUSY = pl.CostEstimate(flops=10**10, transcendentals=0, bytes_accessed=0)
QUICK = pl.CostEstimate(flops=10**6, transcendentals=0, bytes_accessed=0)
WHOLE = pl.BlockSpec(memory_space=pltpu.VMEM)


def expert_rows(rows_in, rows_grad, gate_w, up_w, down_w):
    gate_pre = jnp.dot(rows_in, gate_w, preferred_element_type=F32)
    up_pre = jnp.dot(rows_in, up_w, preferred_element_type=F32)
    squash = jax.nn.sigmoid(gate_pre)
    swish = gate_pre * squash
    hidden = (swish * up_pre).astype(BF16)
    hidden_grad = lax.dot_general(
        rows_grad, down_w, (((1,), (1,)), ((), ())), preferred_element_type=F32
    )
    gate_grad = (hidden_grad * up_pre * squash * (1.0 + gate_pre * (1.0 - squash))).astype(BF16)
    up_grad = (hidden_grad * swish).astype(BF16)
    first = lax.dot_general(
        gate_grad, gate_w, (((1,), (1,)), ((), ())), preferred_element_type=F32
    )
    second = lax.dot_general(up_grad, up_w, (((1,), (1,)), ((), ())), preferred_element_type=F32)
    partial_rows = (first + second).astype(BF16)
    weight_grad = lax.dot_general(
        hidden, rows_grad, (((0,), (0,)), ((), ())), preferred_element_type=F32
    )
    return (partial_rows, weight_grad)


def routed(activations, out_grad, route_weights, expert_ids, w_gate, w_up, w_down):
    n_expert = lax.axis_size("ep")
    n_group = lax.axis_size("sp")
    tok_dev = activations.shape[1]
    width = activations.shape[2]
    capacity = max(2, tok_dev * n_group * TOP * 3 // (2 * n_expert))
    group_ids = lax.all_gather(expert_ids, "sp", axis=1, tiled=True)
    group_in, group_grad, group_weight = (
        lax.all_gather(activations, "sp", axis=1, tiled=True),
        lax.all_gather(out_grad, "sp", axis=1, tiled=True),
        lax.all_gather(route_weights, "sp", axis=1, tiled=True),
    )
    tok_grp = group_ids.shape[1]
    slot_expert = group_ids[0].reshape(-1)
    slot_token = jnp.arange(slot_expert.shape[0], dtype=jnp.int32) // TOP
    onehot = (slot_expert[:, None] == jnp.arange(n_expert, dtype=jnp.int32)[None, :]).astype(
        jnp.int32
    )
    before = jnp.cumsum(onehot, axis=0) - onehot
    rank = jnp.sum(before * onehot, axis=1)
    position = slot_expert * capacity + rank
    total_rows = n_expert * capacity
    token_in = group_in[0][slot_token]
    scaled = (
        group_weight[0].reshape(-1).astype(F32)[:, None] * group_grad[0][slot_token].astype(F32)
    ).astype(BF16)
    send_in = (
        jnp.zeros((total_rows, width), BF16)
        .at[position]
        .set(token_in)
        .reshape(n_expert, capacity, width)
    )
    send_grad = (
        jnp.zeros((total_rows, width), BF16)
        .at[position]
        .set(scaled)
        .reshape(n_expert, capacity, width)
    )
    recv_in, recv_grad = (
        lax.all_to_all(send_in, "ep", split_axis=0, concat_axis=0, tiled=True),
        lax.all_to_all(send_grad, "ep", split_axis=0, concat_axis=0, tiled=True),
    )
    flat_in = recv_in.reshape(total_rows, width)
    flat_grad = recv_grad.reshape(total_rows, width)
    partial_rows, weight_grad = expert_rows(flat_in, flat_grad, w_gate[0], w_up[0], w_down[0])
    partial_rows = partial_rows.reshape(n_expert, capacity, width)
    slot_owner = jnp.full((total_rows,), -1, jnp.int32).at[position].set(slot_token)
    owner_match = jnp.arange(tok_grp, dtype=jnp.int32)[:, None] == slot_owner[None, :]
    back_rows = lax.all_to_all(partial_rows, "ep", split_axis=0, concat_axis=0, tiled=True)
    token_sum = jnp.dot(
        owner_match.astype(BF16),
        back_rows.reshape(total_rows, width),
        preferred_element_type=F32,
    )
    own_sum = lax.psum_scatter(token_sum.astype(BF16), "sp", scatter_dimension=0, tiled=True)
    return (own_sum.reshape(1, tok_dev, width), weight_grad[None])


def back_order(far):
    return far[:1] + far[-1:] + far[1:-1] if len(far) > 1 else far


def exchange(value, partner, n_sp, n_ep):
    pairs = [(i, partner(i)) for i in range(n_sp * n_ep)]
    return lax.ppermute(value, ("sp", "ep"), pairs)


def pack_kernel(in_ref, grad_ref, weight_ref, ids_ref, out_ref, rows, weights, ids, sem):
    tok_dev, width = in_ref.shape[1:]
    copies = [
        pltpu.make_async_copy(source, target, sem.at[n])
        for n, (source, target) in enumerate(
            (
                (weight_ref, weights),
                (ids_ref, ids),
                (in_ref.at[0], rows.at[0]),
                (grad_ref.at[0], rows.at[1]),
            )
        )
    ]
    for copy in copies:
        copy.start()
    for copy in copies:
        copy.wait()
    lane = lax.broadcasted_iota(jnp.int32, (tok_dev, out_ref.shape[1] - width), 1)
    weight = weights[0].astype(F32)
    spread = jnp.zeros(lane.shape, F32)
    for k in range(ids.shape[2]):
        spread += jnp.where(lane == ids[0, :, k : k + 1], weight[:, k : k + 1], 0.0)
    out_ref[:tok_dev, :width] = rows[0]
    out_ref[:tok_dev, width:] = jnp.zeros(lane.shape, BF16)
    out_ref[tok_dev:, :width] = rows[1]
    out_ref[tok_dev:, width:] = spread.astype(BF16)


def pack(activations, out_grad, route_weights, expert_ids, n_expert):
    _, tok_dev, width = out_grad.shape
    operands = (activations, out_grad, route_weights, expert_ids)
    return pl.pallas_call(
        pack_kernel,
        out_shape=jax.ShapeDtypeStruct((2 * tok_dev, width + n_expert + -n_expert % 128), BF16),
        in_specs=[pl.BlockSpec(memory_space=pltpu.HBM)] * 4,
        out_specs=WHOLE,
        scratch_shapes=[
            pltpu.VMEM((2, tok_dev, width), BF16),
            pltpu.VMEM(route_weights.shape, route_weights.dtype),
            pltpu.VMEM(expert_ids.shape, expert_ids.dtype),
            pltpu.SemaphoreType.DMA((4,)),
        ],
        compiler_params=room(2),
        cost_estimate=BUSY,
        name="pack",
    )(*(pltpu.with_memory_space_constraint(x, pltpu.HBM) for x in operands))


def split_kernel(*refs):
    all_ref, in_ref, grad_ref = refs[-3:]
    _, rows, width = in_ref.shape
    for n, ref in enumerate(refs[:-3]):
        all_ref[2 * n * rows : 2 * (n + 1) * rows, :] = ref[...]
        in_ref[n] = ref[:rows, :width]
        grad_ref[n] = ref[rows:, :]


def split(blocks, width):
    rows, wide = blocks[0].shape
    n, half = len(blocks), rows // 2
    return pl.pallas_call(
        split_kernel,
        out_shape=(
            jax.ShapeDtypeStruct((n * rows, wide), BF16),
            jax.ShapeDtypeStruct((n, half, width), BF16),
            jax.ShapeDtypeStruct((n, half, wide), BF16),
        ),
        in_specs=[WHOLE] * n,
        out_specs=(WHOLE,) * 3,
        compiler_params=room(2),
        cost_estimate=QUICK,
        name="split",
    )(*blocks)


def place(pieces, skip, rows):
    tok_dev, width = pieces[2].shape[1], rows.shape[1]
    start = 0

    def put(block):
        nonlocal start
        rows[start : start + tok_dev, :] = block
        start += tok_dev

    def packed(ref, n):
        first = n * 2 * tok_dev + skip
        return ref[first : first + tok_dev, :width]

    for k in range(0, len(pieces), 5):
        near, near_two, both, second, corner = pieces[k : k + 5]
        per = corner.shape[0]
        for p in range(2):
            put(packed(near, p))
            for n in range(per):
                put(both[p * per + n])
        put(packed(near_two, 0))
        for n in range(per):
            put(packed(second, n))
        put(packed(near_two, 1))
        for n in range(per):
            put(corner[n])


def lay_kernel(*refs):
    place(refs[:-1], 0, refs[-1])


def lay(pieces, rows):
    return pl.pallas_call(
        lay_kernel,
        out_shape=jax.ShapeDtypeStruct((rows, pieces[2].shape[2]), BF16),
        in_specs=[WHOLE] * len(pieces),
        out_specs=WHOLE,
        compiler_params=room(4),
        cost_estimate=QUICK,
        name="lay",
    )(*pieces)


def turn_kernel(n, *refs):
    for source, target in zip(refs[:n], refs[n:]):
        for c in range(0, source.shape[0], TURN):
            rows = slice(c, min(c + TURN, source.shape[0]))
            target[:, rows] = source[rows, :].T


def turn(*weights):
    n = len(weights)
    return pl.pallas_call(
        functools.partial(turn_kernel, n),
        out_shape=[jax.ShapeDtypeStruct(w.shape[::-1], w.dtype) for w in weights],
        in_specs=[WHOLE] * n,
        out_specs=[WHOLE] * n,
        compiler_params=room(16),
        cost_estimate=QUICK,
        name="turn",
    )(*weights)


def forward_kernel(rows, gate_w, up_w, gate_by, up_by, hidden_t):
    step = min(256, gate_w.shape[1])
    for c in range(0, gate_w.shape[1], step):
        cols = slice(c, c + step)
        gate_pre = jnp.dot(rows[...], gate_w[:, cols], preferred_element_type=F32)
        up_pre = jnp.dot(rows[...], up_w[:, cols], preferred_element_type=F32)
        squash = jax.nn.sigmoid(gate_pre)
        swish = gate_pre * squash
        gate_by[:, cols] = up_pre * squash * (1.0 + gate_pre * (1.0 - squash))
        up_by[:, cols] = swish
        hidden_t[cols, :] = (swish * up_pre).T.astype(BF16)


def backward_kernel(n, width, *refs):
    pieces, refs = refs[:n], refs[n:]
    down_t, gate_t, up_t, gate_by, up_by, scaled, own, *others, placed = refs
    place(pieces, pieces[2].shape[1], placed)
    expert = lax.axis_index("ep")
    spread = placed[:, width:].astype(F32)
    lane = lax.broadcasted_iota(jnp.int32, spread.shape, 1)
    weight = jnp.sum(jnp.where(lane == expert, spread, 0.0), axis=1, keepdims=True)
    scaled[...] = (weight * placed[:, :width].astype(F32)).astype(BF16)
    hidden_grad = jnp.dot(scaled[...], down_t[...], preferred_element_type=F32)
    gate_grad = (hidden_grad * gate_by[...]).astype(BF16)
    up_grad = (hidden_grad * up_by[...]).astype(BF16)
    kept = own.shape[0]
    step = 256 if width % 256 == 0 else width
    for c in range(0, width, step):
        cols = slice(c, c + step)
        first = jnp.dot(gate_grad, gate_t[:, cols], preferred_element_type=F32)
        second = jnp.dot(up_grad, up_t[:, cols], preferred_element_type=F32)
        part = (first + second).astype(BF16)
        own[:, cols] = part[:kept]
        start = kept
        for other in others:
            other[:, cols] = part[start : start + other.shape[0]]
            start += other.shape[0]


def backward(pieces, down_t, gate_t, up_t, gate_by, up_by):
    n = len(pieces)
    rows = gate_by.shape[0]
    width = down_t.shape[0]
    return pl.pallas_call(
        functools.partial(backward_kernel, n, width),
        out_shape=(
            jax.ShapeDtypeStruct((rows, width), BF16),
            jax.ShapeDtypeStruct((rows // 2, width), BF16),
            jax.ShapeDtypeStruct((rows * 3 // 8, width), BF16),
            jax.ShapeDtypeStruct((rows // 8, width), BF16),
        ),
        in_specs=[WHOLE] * (n + 5),
        out_specs=(WHOLE,) * 4,
        scratch_shapes=[pltpu.VMEM((rows, pieces[2].shape[2]), BF16)],
        compiler_params=room(24),
        cost_estimate=QUICK,
        name="backward",
    )(*pieces, down_t, gate_t, up_t, gate_by, up_by)


def outer_kernel(start, hidden_t, scaled, *refs):
    out, buffer, sem = refs[-3:]
    chunks, size = buffer.shape[:2]
    copies = []
    for n in range(chunks):
        rows = pl.ds(start + n * size, size)
        buffer[n] = jnp.dot(hidden_t[rows, :], scaled[...], preferred_element_type=F32)
        copies.append(pltpu.make_async_copy(buffer.at[n], out.at[rows], sem.at[n]))
        copies[-1].start()
    for copy in copies:
        copy.wait()


def outer(start, chunks, hidden_t, scaled, *so_far):
    units, width = hidden_t.shape[0], scaled.shape[1]
    return pl.pallas_call(
        functools.partial(outer_kernel, start * (units // 8)),
        out_shape=pltpu.HBM((units, width), F32),
        in_specs=[WHOLE] * 2 + [pl.BlockSpec(memory_space=pltpu.HBM)] * len(so_far),
        out_specs=pl.BlockSpec(memory_space=pltpu.HBM),
        scratch_shapes=[
            pltpu.VMEM((chunks, units // 8, width), F32),
            pltpu.SemaphoreType.DMA((chunks,)),
        ],
        input_output_aliases={2: 0} if so_far else {},
        compiler_params=room(12),
        cost_estimate=QUICK,
        name="outer",
    )(hidden_t, scaled, *so_far)


def add_kernel(starts, *refs):
    out = refs[-1]
    rows = out.shape[0]
    total = sum(ref[n : n + rows, :].astype(F32) for n, ref in zip(starts, refs))
    out[...] = total.astype(BF16)


def add_rows(rows, *terms):
    return pl.pallas_call(
        functools.partial(add_kernel, [start for _, start in terms]),
        out_shape=jax.ShapeDtypeStruct((rows, terms[0][0].shape[1]), BF16),
        in_specs=[WHOLE] * len(terms),
        out_specs=WHOLE,
        compiler_params=room(4),
        cost_estimate=QUICK,
        name="add",
    )(*(array for array, _ in terms))


def dense(activations, out_grad, route_weights, expert_ids, w_gate, w_up, w_down):
    n_ep = lax.axis_size("ep")
    n_sp = lax.axis_size("sp")
    tok_dev, width = activations.shape[1:]
    units = w_gate.shape[2]

    def swap(value, partner):
        return exchange(value, partner, n_sp, n_ep)

    far = [4 * j for j in range(1, n_ep // 4)][::-1]
    one = lambda i: i ^ n_ep if i & 1 else i ^ 2
    two = lambda i: i ^ 2 if i & 1 else i ^ n_ep
    core = lambda i: i ^ 1

    mine = pack(activations, out_grad, route_weights, expert_ids, n_ep)
    blocks = {j: swap(mine, lambda i, j=j: i ^ j) for j in far}
    near = jnp.concatenate([mine, swap(mine, one)], axis=0)
    near_two = swap(near, two)
    near = (near, swap(near, core))
    near_two = (near_two, swap(near_two, core))
    all_far, far_in, far_grad = split([blocks[j] for j in sorted(far)], width)
    second = swap(all_far, two)
    second = (second, swap(second, core))

    def gather(column):
        first = swap(column, one)
        both = jnp.concatenate([column, first], axis=0)
        both = (both, swap(both, core))
        corner = swap(first, two)
        corner = (corner, swap(corner, core))
        return [x[k] for k in range(2) for x in (near, near_two, both, second, corner)]

    rows_in = gather(far_in)
    rows_grad = gather(far_grad)
    gate_w, up_w = w_gate[0], w_up[0]
    gate_t, up_t = turn(gate_w, up_w)
    (down_t,) = turn(w_down[0])
    rows = tok_dev * n_ep * n_sp
    placed = lay(rows_in, rows)

    gate_by, up_by, hidden_t = pl.pallas_call(
        forward_kernel,
        out_shape=(
            jax.ShapeDtypeStruct((rows, units), F32),
            jax.ShapeDtypeStruct((rows, units), F32),
            jax.ShapeDtypeStruct((units, rows), BF16),
        ),
        in_specs=[WHOLE] * 3,
        out_specs=(WHOLE,) * 3,
        compiler_params=room(16),
        cost_estimate=QUICK,
        name="forward",
    )(placed, gate_w, up_w)
    scaled, kept, other, other_corner = backward(
        rows_grad, down_t, gate_t, up_t, gate_by, up_by
    )
    weight_grad = ()
    for start, chunks in ((0, 2), (2, 2), (4, 4)):
        weight_grad = (outer(start, chunks, hidden_t, scaled, *weight_grad),)
    weight_grad = weight_grad[0]

    size = kept.shape[0] // 4
    got = swap(other_corner, core)
    corner = add_rows(size, (kept, 3 * size), (got, 0))
    passed = swap(corner, two)
    got = swap(other, core)
    second = add_rows(size, (kept, 2 * size), (got, 2 * size))
    second = swap(second, two)
    first = add_rows(size, (kept, size), (got, size), (passed, 0))
    first = swap(first, one)
    total = kept[:size].astype(F32) + got[:size].astype(F32)
    total = total + second.astype(F32) + first.astype(F32)
    sent = total.astype(BF16)
    own = total[:tok_dev]
    for j in back_order(far):
        block = sent[j // 4 * tok_dev : (j // 4 + 1) * tok_dev]
        own = own + swap(block, lambda i, j=j: i ^ j).astype(F32)
    return (own.astype(BF16)[None], weight_grad[None])


def per_device(activations, out_grad, route_weights, expert_ids, w_gate, w_up, w_down):
    n_ep = lax.axis_size("ep")
    n_sp = lax.axis_size("sp")
    tokens = activations.shape[1] * n_sp * n_ep
    rows = n_ep * max(2, activations.shape[1] * n_sp * TOP * 3 // (2 * n_ep))
    few = tokens <= 2 * rows and n_sp == 2 and n_ep >= 8 and n_ep & (n_ep - 1) == 0
    if not few:
        return routed(activations, out_grad, route_weights, expert_ids, w_gate, w_up, w_down)
    return dense(activations, out_grad, route_weights, expert_ids, w_gate, w_up, w_down)


def solution(mesh):
    return jax.shard_map(
        per_device,
        mesh=mesh,
        in_specs=(
            P("ep", "sp", None),
            P("ep", "sp", None),
            P("ep", "sp", None),
            P("ep", "sp", None),
            P("ep", None, "sp"),
            P("ep", None, "sp"),
            P("ep", "sp", None),
        ),
        out_specs=(P("ep", "sp", None), P("ep", "sp", None)),
        check_vma=False,
    )
```

```python
import functools

import jax
import jax.numpy as jnp
from jax import lax
from jax.experimental import pallas as pl
from jax.experimental.pallas import tpu as pltpu
from jax.sharding import PartitionSpec as P

TOP = 8
TURN = 512
F32 = jnp.float32
BF16 = jnp.bfloat16


def room(mib):
    return pltpu.CompilerParams(vmem_limit_bytes=mib * 2**20)


BUSY = pl.CostEstimate(flops=10**10, transcendentals=0, bytes_accessed=0)
QUICK = pl.CostEstimate(flops=10**6, transcendentals=0, bytes_accessed=0)
WHOLE = pl.BlockSpec(memory_space=pltpu.VMEM)


def expert_rows(rows_in, rows_grad, gate_w, up_w, down_w):
    gate_pre = jnp.dot(rows_in, gate_w, preferred_element_type=F32)
    up_pre = jnp.dot(rows_in, up_w, preferred_element_type=F32)
    squash = jax.nn.sigmoid(gate_pre)
    swish = gate_pre * squash
    hidden = (swish * up_pre).astype(BF16)
    hidden_grad = lax.dot_general(
        rows_grad, down_w, (((1,), (1,)), ((), ())), preferred_element_type=F32
    )
    gate_grad = (hidden_grad * up_pre * squash * (1.0 + gate_pre * (1.0 - squash))).astype(BF16)
    up_grad = (hidden_grad * swish).astype(BF16)
    first = lax.dot_general(
        gate_grad, gate_w, (((1,), (1,)), ((), ())), preferred_element_type=F32
    )
    second = lax.dot_general(up_grad, up_w, (((1,), (1,)), ((), ())), preferred_element_type=F32)
    partial_rows = (first + second).astype(BF16)
    weight_grad = lax.dot_general(
        hidden, rows_grad, (((0,), (0,)), ((), ())), preferred_element_type=F32
    )
    return (partial_rows, weight_grad)


def routed(activations, out_grad, route_weights, expert_ids, w_gate, w_up, w_down):
    n_expert = lax.axis_size("ep")
    n_group = lax.axis_size("sp")
    tok_dev = activations.shape[1]
    width = activations.shape[2]
    capacity = max(2, tok_dev * n_group * TOP * 3 // (2 * n_expert))
    group_ids = lax.all_gather(expert_ids, "sp", axis=1, tiled=True)
    group_in, group_grad, group_weight = (
        lax.all_gather(activations, "sp", axis=1, tiled=True),
        lax.all_gather(out_grad, "sp", axis=1, tiled=True),
        lax.all_gather(route_weights, "sp", axis=1, tiled=True),
    )
    tok_grp = group_ids.shape[1]
    slot_expert = group_ids[0].reshape(-1)
    slot_token = jnp.arange(slot_expert.shape[0], dtype=jnp.int32) // TOP
    onehot = (slot_expert[:, None] == jnp.arange(n_expert, dtype=jnp.int32)[None, :]).astype(
        jnp.int32
    )
    before = jnp.cumsum(onehot, axis=0) - onehot
    rank = jnp.sum(before * onehot, axis=1)
    position = slot_expert * capacity + rank
    total_rows = n_expert * capacity
    token_in = group_in[0][slot_token]
    scaled = (
        group_weight[0].reshape(-1).astype(F32)[:, None] * group_grad[0][slot_token].astype(F32)
    ).astype(BF16)
    send_in = (
        jnp.zeros((total_rows, width), BF16)
        .at[position]
        .set(token_in)
        .reshape(n_expert, capacity, width)
    )
    send_grad = (
        jnp.zeros((total_rows, width), BF16)
        .at[position]
        .set(scaled)
        .reshape(n_expert, capacity, width)
    )
    recv_in, recv_grad = (
        lax.all_to_all(send_in, "ep", split_axis=0, concat_axis=0, tiled=True),
        lax.all_to_all(send_grad, "ep", split_axis=0, concat_axis=0, tiled=True),
    )
    flat_in = recv_in.reshape(total_rows, width)
    flat_grad = recv_grad.reshape(total_rows, width)
    partial_rows, weight_grad = expert_rows(flat_in, flat_grad, w_gate[0], w_up[0], w_down[0])
    partial_rows = partial_rows.reshape(n_expert, capacity, width)
    slot_owner = jnp.full((total_rows,), -1, jnp.int32).at[position].set(slot_token)
    owner_match = jnp.arange(tok_grp, dtype=jnp.int32)[:, None] == slot_owner[None, :]
    back_rows = lax.all_to_all(partial_rows, "ep", split_axis=0, concat_axis=0, tiled=True)
    token_sum = jnp.dot(
        owner_match.astype(BF16),
        back_rows.reshape(total_rows, width),
        preferred_element_type=F32,
    )
    own_sum = lax.psum_scatter(token_sum.astype(BF16), "sp", scatter_dimension=0, tiled=True)
    return (own_sum.reshape(1, tok_dev, width), weight_grad[None])


def back_order(far):
    return far[:1] + far[-1:] + far[1:-1] if len(far) > 1 else far


def exchange(value, partner, n_sp, n_ep):
    pairs = [(i, partner(i)) for i in range(n_sp * n_ep)]
    return lax.ppermute(value, ("sp", "ep"), pairs)


def pack_kernel(in_ref, grad_ref, weight_ref, ids_ref, out_ref, rows, weights, ids, sem):
    tok_dev, width = in_ref.shape[1:]
    copies = [
        pltpu.make_async_copy(source, target, sem.at[n])
        for n, (source, target) in enumerate(
            (
                (weight_ref, weights),
                (ids_ref, ids),
                (in_ref.at[0], rows.at[0]),
                (grad_ref.at[0], rows.at[1]),
            )
        )
    ]
    for copy in copies:
        copy.start()
    for copy in copies:
        copy.wait()
    lane = lax.broadcasted_iota(jnp.int32, (tok_dev, out_ref.shape[1] - width), 1)
    weight = weights[0].astype(F32)
    spread = jnp.zeros(lane.shape, F32)
    for k in range(ids.shape[2]):
        spread += jnp.where(lane == ids[0, :, k : k + 1], weight[:, k : k + 1], 0.0)
    out_ref[:tok_dev, :width] = rows[0]
    out_ref[:tok_dev, width:] = jnp.zeros(lane.shape, BF16)
    out_ref[tok_dev:, :width] = rows[1]
    out_ref[tok_dev:, width:] = spread.astype(BF16)


def pack(activations, out_grad, route_weights, expert_ids, n_expert):
    _, tok_dev, width = out_grad.shape
    operands = (activations, out_grad, route_weights, expert_ids)
    return pl.pallas_call(
        pack_kernel,
        out_shape=jax.ShapeDtypeStruct((2 * tok_dev, width + n_expert + -n_expert % 128), BF16),
        in_specs=[pl.BlockSpec(memory_space=pltpu.HBM)] * 4,
        out_specs=WHOLE,
        scratch_shapes=[
            pltpu.VMEM((2, tok_dev, width), BF16),
            pltpu.VMEM(route_weights.shape, route_weights.dtype),
            pltpu.VMEM(expert_ids.shape, expert_ids.dtype),
            pltpu.SemaphoreType.DMA((4,)),
        ],
        compiler_params=room(2),
        cost_estimate=BUSY,
        name="pack",
    )(*(pltpu.with_memory_space_constraint(x, pltpu.HBM) for x in operands))


def split_kernel(*refs):
    all_ref, in_ref, grad_ref = refs[-3:]
    _, rows, width = in_ref.shape
    for n, ref in enumerate(refs[:-3]):
        all_ref[2 * n * rows : 2 * (n + 1) * rows, :] = ref[...]
        in_ref[n] = ref[:rows, :width]
        grad_ref[n] = ref[rows:, :]


def split(blocks, width):
    rows, wide = blocks[0].shape
    n, half = len(blocks), rows // 2
    return pl.pallas_call(
        split_kernel,
        out_shape=(
            jax.ShapeDtypeStruct((n * rows, wide), BF16),
            jax.ShapeDtypeStruct((n, half, width), BF16),
            jax.ShapeDtypeStruct((n, half, wide), BF16),
        ),
        in_specs=[WHOLE] * n,
        out_specs=(WHOLE,) * 3,
        compiler_params=room(2),
        cost_estimate=QUICK,
        name="split",
    )(*blocks)


def place(blocks, rows):
    start = 0
    for block in blocks:
        rows[start : start + block.shape[0], :] = block
        start += block.shape[0]


def packed(ref, n, like, skip):
    tok_dev, width = like.shape[1:]
    first = n * 2 * tok_dev + skip
    return ref[first : first + tok_dev, :width]


def first_columns(pieces, skip):
    for k in range(0, len(pieces), 4):
        near, near_two, both, second = pieces[k : k + 4]
        per = both.shape[0] // 2
        for p in range(2):
            yield packed(near, p, both, skip)
            for n in range(per):
                yield both[p * per + n]
        yield packed(near_two, 0, both, skip)
        for n in range(per):
            yield packed(second, n, both, skip)


def last_columns(pieces, skip):
    for k in range(0, len(pieces), 2):
        near_two, corner = pieces[k : k + 2]
        yield packed(near_two, 1, corner, skip)
        for n in range(corner.shape[0]):
            yield corner[n]


def merged(early, late):
    n, m = early.shape[0] // 2, late.shape[0] // 2
    return jnp.concatenate([early[:n], late[:m], early[n:], late[m:]], axis=0)


def scaled_rows(placed, width):
    spread = placed[:, width:].astype(F32)
    lane = lax.broadcasted_iota(jnp.int32, spread.shape, 1)
    weight = jnp.sum(jnp.where(lane == lax.axis_index("ep"), spread, 0.0), axis=1, keepdims=True)
    return (weight * placed[:, :width].astype(F32)).astype(BF16)


def lay_in_kernel(*refs):
    *pieces, out = refs
    own, corner, other = pieces[:4], pieces[4], pieces[5:]
    blocks = list(first_columns(own, 0)) + list(last_columns((own[1], corner), 0))
    place(blocks + list(first_columns(other, 0)), out)


def lay(kernel, pieces, width, columns):
    rows = (pieces[2].shape[0] // 2 + 1) * pieces[2].shape[1] * columns
    return pl.pallas_call(
        kernel,
        out_shape=jax.ShapeDtypeStruct((rows, width), BF16),
        in_specs=[WHOLE] * len(pieces),
        out_specs=WHOLE,
        compiler_params=room(4),
        cost_estimate=QUICK,
        name="lay",
    )(*pieces)


def turn_kernel(n, *refs):
    for source, target in zip(refs[:n], refs[n:]):
        for c in range(0, source.shape[0], TURN):
            rows = slice(c, min(c + TURN, source.shape[0]))
            target[:, rows] = source[rows, :].T


def turn(*weights):
    n = len(weights)
    return pl.pallas_call(
        functools.partial(turn_kernel, n),
        out_shape=[jax.ShapeDtypeStruct(w.shape[::-1], w.dtype) for w in weights],
        in_specs=[WHOLE] * n,
        out_specs=[WHOLE] * n,
        compiler_params=room(16),
        cost_estimate=QUICK,
        name="turn",
    )(*weights)


def forward_kernel(n, early, *refs):
    pieces, (gate_w, up_w, gate_by, up_by, hidden_t, late) = refs[:n], refs[n:]
    place(last_columns(pieces, 0), late)
    rows = jnp.concatenate([early[...], late[...]], axis=0)
    step = min(256, gate_w.shape[1])
    for c in range(0, gate_w.shape[1], step):
        cols = slice(c, c + step)
        gate_pre = jnp.dot(rows, gate_w[:, cols], preferred_element_type=F32)
        up_pre = jnp.dot(rows, up_w[:, cols], preferred_element_type=F32)
        squash = jax.nn.sigmoid(gate_pre)
        swish = gate_pre * squash
        gate_by[:, cols] = up_pre * squash * (1.0 + gate_pre * (1.0 - squash))
        up_by[:, cols] = swish
        hidden_t[cols, :] = (swish * up_pre).T.astype(BF16)


def backward_kernel(n, m, width, *refs):
    firsts, lasts, refs = refs[:n], refs[n : n + m], refs[n + m :]
    down_t, gate_t, up_t, gate_by, up_by, scaled, own, *others, early, late = refs
    skip = lasts[1].shape[1]
    place(first_columns(firsts, skip), early)
    place(last_columns(lasts, skip), late)
    scaled[...] = merged(scaled_rows(early, width), scaled_rows(late, width))
    hidden_grad = jnp.dot(scaled[...], down_t[...], preferred_element_type=F32)
    gate_grad = (hidden_grad * gate_by[...]).astype(BF16)
    up_grad = (hidden_grad * up_by[...]).astype(BF16)
    kept = own.shape[0]
    step = 256 if width % 256 == 0 else width
    for c in range(0, width, step):
        cols = slice(c, c + step)
        first = jnp.dot(gate_grad, gate_t[:, cols], preferred_element_type=F32)
        second = jnp.dot(up_grad, up_t[:, cols], preferred_element_type=F32)
        part = (first + second).astype(BF16)
        own[:, cols] = part[:kept]
        start = kept
        for other in others:
            other[:, cols] = part[start : start + other.shape[0]]
            start += other.shape[0]


def backward(early, pieces, down_t, gate_t, up_t, gate_by, up_by):
    n, m = len(early), len(pieces)
    rows = gate_by.shape[0]
    width = down_t.shape[0]
    return pl.pallas_call(
        functools.partial(backward_kernel, n, m, width),
        out_shape=(
            jax.ShapeDtypeStruct((rows, width), BF16),
            jax.ShapeDtypeStruct((rows // 2, width), BF16),
            jax.ShapeDtypeStruct((rows * 3 // 8, width), BF16),
            jax.ShapeDtypeStruct((rows // 8, width), BF16),
        ),
        in_specs=[WHOLE] * (n + m + 5),
        out_specs=(WHOLE,) * 4,
        scratch_shapes=[
            pltpu.VMEM((rows * 3 // 4, pieces[1].shape[2]), BF16),
            pltpu.VMEM((rows // 4, pieces[1].shape[2]), BF16),
        ],
        compiler_params=room(24),
        cost_estimate=QUICK,
        name="backward",
    )(*early, *pieces, down_t, gate_t, up_t, gate_by, up_by)


def outer_kernel(start, hidden_t, scaled, *refs):
    out, buffer, sem = refs[-3:]
    chunks, size = buffer.shape[:2]
    copies = []
    for n in range(chunks):
        rows = pl.ds(start + n * size, size)
        buffer[n] = jnp.dot(hidden_t[rows, :], scaled[...], preferred_element_type=F32)
        copies.append(pltpu.make_async_copy(buffer.at[n], out.at[rows], sem.at[n]))
        copies[-1].start()
    for copy in copies:
        copy.wait()


def outer(start, chunks, hidden_t, scaled, *so_far):
    units, width = hidden_t.shape[0], scaled.shape[1]
    return pl.pallas_call(
        functools.partial(outer_kernel, start * (units // 8)),
        out_shape=pltpu.HBM((units, width), F32),
        in_specs=[WHOLE] * 2 + [pl.BlockSpec(memory_space=pltpu.HBM)] * len(so_far),
        out_specs=pl.BlockSpec(memory_space=pltpu.HBM),
        scratch_shapes=[
            pltpu.VMEM((chunks, units // 8, width), F32),
            pltpu.SemaphoreType.DMA((chunks,)),
        ],
        input_output_aliases={2: 0} if so_far else {},
        compiler_params=room(12),
        cost_estimate=QUICK,
        name="outer",
    )(hidden_t, scaled, *so_far)


def add_kernel(starts, *refs):
    out = refs[-1]
    rows = out.shape[0]
    total = sum(ref[n : n + rows, :].astype(F32) for n, ref in zip(starts, refs))
    out[...] = total.astype(BF16)


def add_rows(rows, *terms):
    return pl.pallas_call(
        functools.partial(add_kernel, [start for _, start in terms]),
        out_shape=jax.ShapeDtypeStruct((rows, terms[0][0].shape[1]), BF16),
        in_specs=[WHOLE] * len(terms),
        out_specs=WHOLE,
        compiler_params=room(4),
        cost_estimate=QUICK,
        name="add",
    )(*(array for array, _ in terms))


def dense(activations, out_grad, route_weights, expert_ids, w_gate, w_up, w_down):
    n_ep = lax.axis_size("ep")
    n_sp = lax.axis_size("sp")
    tok_dev, width = activations.shape[1:]
    units = w_gate.shape[2]

    def swap(value, partner):
        return exchange(value, partner, n_sp, n_ep)

    far = [4 * j for j in range(1, n_ep // 4)][::-1]
    one = lambda i: i ^ n_ep if i & 1 else i ^ 2
    two = lambda i: i ^ 2 if i & 1 else i ^ n_ep
    core = lambda i: i ^ 1

    mine = pack(activations, out_grad, route_weights, expert_ids, n_ep)
    blocks = {j: swap(mine, lambda i, j=j: i ^ j) for j in far}
    near = jnp.concatenate([mine, swap(mine, one)], axis=0)
    near_two = swap(near, two)
    near = (near, swap(near, core))
    near_two = (near_two, swap(near_two, core))
    all_far, far_in, far_grad = split([blocks[j] for j in sorted(far)], width)
    second = swap(all_far, two)
    second = (second, swap(second, core))

    def gather(column):
        first = swap(column, one)
        both = jnp.concatenate([column, first], axis=0)
        both = (both, swap(both, core))
        corner = swap(first, two)
        corner = (corner, swap(corner, core))
        early = [x[k] for k in range(2) for x in (near, near_two, both, second)]
        return early, [x[k] for k in range(2) for x in (near_two, corner)]

    early_in, late_in = gather(far_in)
    early_grad, late_grad = gather(far_grad)
    gate_w, up_w = w_gate[0], w_up[0]
    gate_t, up_t = turn(gate_w, up_w)
    (down_t,) = turn(w_down[0])
    rows = tok_dev * n_ep * n_sp
    early_in = early_in[:4] + late_in[1:2] + early_in[4:]
    early_in = lay(lay_in_kernel, early_in, width, 7)
    late_in = late_in[2:]
    n = len(late_in)

    gate_by, up_by, hidden_t = pl.pallas_call(
        functools.partial(forward_kernel, n),
        out_shape=(
            jax.ShapeDtypeStruct((rows, units), F32),
            jax.ShapeDtypeStruct((rows, units), F32),
            jax.ShapeDtypeStruct((units, rows), BF16),
        ),
        in_specs=[WHOLE] * (n + 3),
        out_specs=(WHOLE,) * 3,
        scratch_shapes=[pltpu.VMEM((rows // 8, width), BF16)],
        compiler_params=room(16),
        cost_estimate=QUICK,
        name="forward",
    )(early_in, *late_in, gate_w, up_w)
    scaled, kept, other, other_corner = backward(
        early_grad, late_grad, down_t, gate_t, up_t, gate_by, up_by
    )
    weight_grad = ()
    for start, chunks in ((0, 2), (2, 2), (4, 4)):
        weight_grad = (outer(start, chunks, hidden_t, scaled, *weight_grad),)
    weight_grad = weight_grad[0]

    size = kept.shape[0] // 4
    got = swap(other_corner, core)
    corner = add_rows(size, (kept, 3 * size), (got, 0))
    passed = swap(corner, two)
    got = swap(other, core)
    second = add_rows(size, (kept, 2 * size), (got, 2 * size))
    second = swap(second, two)
    first = add_rows(size, (kept, size), (got, size), (passed, 0))
    first = swap(first, one)
    total = kept[:size].astype(F32) + got[:size].astype(F32)
    total = total + second.astype(F32) + first.astype(F32)
    sent = total.astype(BF16)
    own = total[:tok_dev]
    for j in back_order(far):
        block = sent[j // 4 * tok_dev : (j // 4 + 1) * tok_dev]
        own = own + swap(block, lambda i, j=j: i ^ j).astype(F32)
    return (own.astype(BF16)[None], weight_grad[None])


def per_device(activations, out_grad, route_weights, expert_ids, w_gate, w_up, w_down):
    n_ep = lax.axis_size("ep")
    n_sp = lax.axis_size("sp")
    tokens = activations.shape[1] * n_sp * n_ep
    rows = n_ep * max(2, activations.shape[1] * n_sp * TOP * 3 // (2 * n_ep))
    few = tokens <= 2 * rows and n_sp == 2 and n_ep >= 8 and n_ep & (n_ep - 1) == 0
    if not few:
        return routed(activations, out_grad, route_weights, expert_ids, w_gate, w_up, w_down)
    return dense(activations, out_grad, route_weights, expert_ids, w_gate, w_up, w_down)


def solution(mesh):
    return jax.shard_map(
        per_device,
        mesh=mesh,
        in_specs=(
            P("ep", "sp", None),
            P("ep", "sp", None),
            P("ep", "sp", None),
            P("ep", "sp", None),
            P("ep", None, "sp"),
            P("ep", None, "sp"),
            P("ep", "sp", None),
        ),
        out_specs=(P("ep", "sp", None), P("ep", "sp", None)),
        check_vma=False,
    )
```
